512 devices in a mesh: rep: 16 (over z, x_hi), grp: 32 (over y, x_lo, core).
Axes of the slice: x: 4 (x_hi: 2, x_lo: 2; x = x_hi * 2 + x_lo), y: 8, z: 8, core: 2. Of those that a mesh axis runs over, the one named last changes fastest.
Arguments:
- features: bfloat16 [65536, 256], P(('rep', 'grp')), may hold values from -6 to 6
- weight: bfloat16 [256, 256], replicated, may hold values from -0.375 to 0.375
- bias: float32 [256], replicated, may hold values from -3 to 3
- cotangent: bfloat16 [65536, 256], P(('rep', 'grp')), may hold values from -6 to 6
- degree: int32 [65536], P(('rep', 'grp')), may hold values from 1 to 99
- tile_cols: int32 [512, 24], P(('rep', 'grp')), may hold values from 0 to 95, as said below
- edge_tile: int32 [512, 3840], P(('rep', 'grp')), may hold values from 0 to 23
- edge_row: int32 [512, 3840], P(('rep', 'grp')), may hold values from 0 to 127
- edge_col: int32 [512, 3840], P(('rep', 'grp')), may hold values from 0 to 127
Outputs:
- hidden: bfloat16 [65536, 256], P(('rep', 'grp'))
- grad_features: bfloat16 [65536, 256], P(('rep', 'grp'))
- grad_weight: float32 [256, 256], replicated
- grad_bias: float32 [256], replicated
The draws below stay inside these ranges and needn't reach their ends.
Inputs may be any that keep to these rules, and one draw needn't show every extreme that they name: `tile_cols`: each row lists 8 different tile columns in each of the ranges 0 to 31, 32 to 63 and 64 to 95, in that order.
All inputs are finite; a program needn't handle non-finite values.
Results may differ from the reference program's by a relative error of at most 0.0062.
Values may be sent and summed in bfloat16 or wider, within the bound.
No kernel may reach another device: no remote copies, remote signals or barrier semaphores. Data moves between devices by JAX's collectives and lax.ppermute only.
A program may use at most 64 MiB of HBM per device.

```python
import jax
import jax.numpy as jnp
from jax import lax

F = 256
TILE = 128
TPB = 8
TCAP = 24
E_DEV = 3840
NODES = 65536
N_REP = 16
N_GRP = 32
DEVICES = 512


def draw_tile_cols(key, part):
    keys = jax.random.split(jax.random.fold_in(key, 17), DEVICES * 3)
    chosen = jax.vmap(lambda one: jax.random.permutation(one, N_GRP)[:TPB])(keys)
    chosen = chosen.reshape(DEVICES, 3, TPB) + (jnp.arange(3, dtype=jnp.int32) * N_GRP)[None, :, None]
    return chosen.reshape(DEVICES, 3 * TPB).astype(jnp.int32)


def with_ends(drawn, stream_key, low, largest):
    longest = drawn.shape.index(max(drawn.shape))
    spots = []
    for shift in (0, 1):
        where = [jax.random.randint(jax.random.fold_in(stream_key, axis), (), 0, length) for axis, length in enumerate(drawn.shape)]
        where[longest] = (where[longest] + shift) % drawn.shape[longest]
        spots.append(tuple(where))
    return drawn.at[spots[0]].set(low).at[spots[1]].set(largest)


def levels(rng, dims, pieces, low, top_value):
    loudness = 1.0
    for dim, shards_of in pieces:
        draws = jax.random.uniform(jax.random.fold_in(jax.random.fold_in(rng, 6), dim), (shards_of,), jnp.float32, low / len(pieces), top_value / len(pieces))
        loudness = loudness * jnp.repeat(jnp.exp(draws), dims[dim] // shards_of).reshape((-1,) + (1,) * (len(dims) - 1 - dim))
    return loudness


def centred(stream_key, shape, scale, bound, pieces=(), held_as=jnp.bfloat16):
    result = jax.random.normal(stream_key, shape, jnp.float32) * scale
    if len(pieces) > 0:
        result = levels(stream_key, shape, pieces, -0.22, 0.18) * result
    return jnp.clip(result, min=-bound, max=bound).astype(held_as)


def setup_inputs(seed: int = 0) -> dict:
    splits = jax.random.split(jax.random.key(seed), 10)
    return {
        "features": centred(splits[0], (NODES, F), 1.0, 6.0, ((0, 512),)),
        "weight": centred(splits[1], (F, F), F ** -0.5, 0.375),
        "bias": centred(splits[2], (F,), 0.5, 3.0, (), jnp.float32),
        "cotangent": centred(splits[3], (NODES, F), 1.0, 6.0, ((0, 512),)),
        "degree": with_ends(jax.random.randint(splits[4], (NODES,), 1, 100), jax.random.fold_in(splits[4], 1), 1, 99).astype(jnp.int32),
        "tile_cols": draw_tile_cols(jax.random.fold_in(splits[9], 71), 0),
        "edge_tile": with_ends(jax.random.randint(splits[6], (DEVICES, E_DEV), 0, TCAP), jax.random.fold_in(splits[6], 1), 0, TCAP - 1).astype(jnp.int32),
        "edge_row": with_ends(jax.random.randint(splits[7], (DEVICES, E_DEV), 0, TILE), jax.random.fold_in(splits[7], 1), 0, TILE - 1).astype(jnp.int32),
        "edge_col": with_ends(jax.random.randint(splits[8], (DEVICES, E_DEV), 0, TILE), jax.random.fold_in(splits[8], 1), 0, TILE - 1).astype(jnp.int32),
    }


def reference(features, weight, bias, cotangent, degree, tile_cols, edge_tile, edge_row, edge_col):
    block = TILE * N_GRP
    dinv = lax.rsqrt(degree.astype(jnp.float32))
    scaled = (jnp.dot(features, weight, preferred_element_type=jnp.float32) * dinv[:, None]).astype(jnp.bfloat16)
    device_ids = jnp.arange(DEVICES, dtype=jnp.int32)
    columns = jnp.take_along_axis(tile_cols, edge_tile, axis=1)
    source_group = (device_ids[:, None] // N_GRP - 1 + columns // N_GRP) % N_REP
    source = (source_group * block + columns % N_GRP * TILE + edge_col).astype(jnp.int32)
    window = (columns * TILE + edge_col).astype(jnp.int32)

    def forward_one(pair):
        sources, rows = pair
        values = scaled[sources].astype(jnp.float32)
        return jax.ops.segment_sum(values, rows, num_segments=TILE)
    sums = lax.map(forward_one, (source, edge_row)).reshape(NODES, F)
    pre = sums * dinv[:, None] + bias[None, :]
    sig = jax.nn.sigmoid(pre)
    hidden = (pre * sig).astype(jnp.bfloat16)
    grad_pre = cotangent.astype(jnp.float32) * sig * (1.0 + pre * (1.0 - sig))
    back = (grad_pre * dinv[:, None]).astype(jnp.bfloat16).reshape(DEVICES, TILE, F)

    def backward_one(total, index):
        rows = edge_row[index]
        values = back[index][rows].astype(jnp.float32)
        part = jax.ops.segment_sum(values, window[index], num_segments=3 * block)
        first = lax.optimization_barrier(part[:block].astype(jnp.bfloat16)).astype(jnp.float32)
        last = lax.optimization_barrier(part[2 * block:].astype(jnp.bfloat16)).astype(jnp.float32)
        group = index // N_GRP
        total = total.at[(group - 1) % N_REP].add(first)
        total = total.at[group].add(part[block:2 * block])
        total = total.at[(group + 1) % N_REP].add(last)
        return (total, None)
    start = jnp.zeros((N_REP, block, F), jnp.float32)
    grad_sum, unused = lax.scan(backward_one, start, device_ids)
    grad_scaled = (grad_sum.reshape(NODES, F) * dinv[:, None]).astype(jnp.bfloat16)
    grad_features = jnp.dot(grad_scaled, weight.T, preferred_element_type=jnp.float32).astype(jnp.bfloat16)
    grad_weight = jnp.dot(features.T, grad_scaled, preferred_element_type=jnp.float32)
    grad_bias = lax.optimization_barrier(jnp.sum(grad_pre, axis=0))
    return (hidden, grad_features, grad_weight, grad_bias)
```

```python
import functools

import jax
import jax.numpy as jnp
from jax import lax
from jax.experimental import pallas as pl
from jax.experimental.pallas import tpu as pltpu
from jax.sharding import PartitionSpec as P

SUB = 8
LANE = 128


def shifted(x, axis, by):
    size = lax.axis_size(axis)
    return lax.ppermute(x, axis, [(i, (i + by) % size) for i in range(size)])


def vmem():
    return pl.BlockSpec(memory_space=pltpu.VMEM)


def smem():
    return pl.BlockSpec(memory_space=pltpu.SMEM)


def count_kernel(chunk, xk_ref, yk_ref, out_ref, acc_ref):
    edges = xk_ref.shape[1]
    tall = acc_ref.shape[0]
    wide = acc_ref.shape[1]
    for step in range(edges // chunk):
        xk = xk_ref[:, pl.ds(step * chunk, chunk)]
        yk = yk_ref[:, pl.ds(step * chunk, chunk)]
        left = (lax.broadcasted_iota(jnp.int32, (tall, chunk), 0) == xk).astype(jnp.float32).astype(jnp.bfloat16)
        right = (lax.broadcasted_iota(jnp.int32, (wide, chunk), 0) == yk).astype(jnp.float32).astype(jnp.bfloat16)
        part = lax.dot_general(left, right, (((1,), (1,)), ((), ())), preferred_element_type=jnp.float32)
        if step == 0:
            acc_ref[...] = part
        else:
            acc_ref[...] += part
    rows = out_ref.shape[0]
    for block in range(tall // rows):
        out_ref[:, pl.ds(block * wide, wide)] = acc_ref[pl.ds(block * rows, rows), :].astype(jnp.bfloat16)


def build_slab(row, key, rows, keys):
    wide = 256
    edges = row.shape[0]
    chunk = 768 if edges % 768 == 0 else 128
    tall = rows * (keys // wide)
    xk = ((key // wide) * rows + row).reshape(1, edges)
    yk = (key % wide).reshape(1, edges)
    return pl.pallas_call(
        functools.partial(count_kernel, chunk),
        out_shape=jax.ShapeDtypeStruct((rows, keys), jnp.bfloat16),
        in_specs=[vmem(), vmem()],
        out_specs=vmem(),
        scratch_shapes=[pltpu.VMEM((tall, wide), jnp.float32)],
        name="count",
    )(xk, yk)


def select_kernel(members, per_part, idx_ref, a_ref, b_ref, c_ref, out_ref):
    listed = 3 * per_part

    def one(d, carry):
        base = d * listed
        for t in range(listed):
            src = (a_ref, b_ref, c_ref)[t // per_part]
            at = jnp.bitwise_and(idx_ref[base + t], members - 1)
            out_ref[base + t] = src[at]
        return carry

    lax.fori_loop(0, members, one, 0)


def select(idx, left, own, right, per_part):
    members = own.shape[0]
    return pl.pallas_call(
        functools.partial(select_kernel, members, per_part),
        out_shape=jax.ShapeDtypeStruct((members * 3 * per_part, SUB, LANE), own.dtype),
        in_specs=[smem(), vmem(), vmem(), vmem()],
        out_specs=vmem(),
        name="select",
    )(idx, left, own, right)


def layer_kernel(listed, slab_ref, x_ref, dinv_ref, bias_ref, cot_ref, hid_ref, part_ref):
    dinv = dinv_ref[...]
    groups = part_ref.shape[1]
    span = listed * SUB
    sums = []
    for half in range(2):
        lanes = slice(half * LANE, (half + 1) * LANE)
        total = jnp.dot(slab_ref[...], x_ref[half], preferred_element_type=jnp.float32)
        pre = total * dinv + bias_ref[:, lanes]
        sig = jax.nn.sigmoid(pre)
        hid_ref[:, lanes] = (pre * sig).astype(hid_ref.dtype)
        grad_pre = cot_ref[:, lanes].astype(jnp.float32) * sig * (1.0 + pre * (1.0 - sig))
        sums.append(jnp.sum(grad_pre, axis=0, keepdims=True))
        back = (grad_pre * dinv).astype(jnp.bfloat16)
        partial = lax.dot_general(
            slab_ref[...], back, (((0,), (0,)), ((), ())), preferred_element_type=jnp.float32
        )
        for a in range(groups):
            piece = partial[a * span : (a + 1) * span, :].reshape(listed, SUB, LANE)
            part_ref[half, a, pl.ds(0, listed)] = piece.astype(jnp.bfloat16)
    high = [s.astype(jnp.bfloat16).astype(jnp.float32) for s in sums]
    low = [s - h for s, h in zip(sums, high)]
    at = lax.broadcasted_iota(jnp.int32, (SUB, LANE), 0)
    extra = jnp.zeros((SUB, LANE), jnp.float32)
    for index, value in enumerate(high + low):
        extra = jnp.where(at == index, value, extra)
    extra = extra.astype(jnp.bfloat16)
    for half in range(2):
        for a in range(groups):
            part_ref[half, a, listed] = extra


def layer(slab, x, dinv, bias, cotangent, listed):
    rows, width = cotangent.shape
    groups = rows // SUB
    return pl.pallas_call(
        functools.partial(layer_kernel, listed),
        out_shape=(
            jax.ShapeDtypeStruct((rows, width), jnp.bfloat16),
            jax.ShapeDtypeStruct((2, groups, listed + 1, SUB, LANE), jnp.bfloat16),
        ),
        in_specs=[vmem()] * 5,
        out_specs=(vmem(), vmem()),
        name="layer",
    )(slab, x, dinv, bias, cotangent)


def collect_kernel(members, per_part, chains, idx_ref, got_ref, prev_ref, own_ref, next_ref, extra_ref, acc_ref):
    listed = 3 * per_part
    acc_ref[...] = jnp.zeros_like(acc_ref)

    def some(step, extra):
        for t in range(listed):
            for j in range(chains):
                d = step * chains + j
                at = jnp.bitwise_and(idx_ref[d * listed + t], members - 1)
                acc_ref[j, t // per_part, at] += got_ref[d, t].astype(jnp.float32)
        for j in range(chains):
            extra = extra + got_ref[step * chains + j, listed].astype(jnp.float32)
        return extra

    extra = lax.fori_loop(0, members // chains, some, jnp.zeros((SUB, LANE), jnp.float32))
    extra_ref[...] = extra
    for k, ref in enumerate((prev_ref, own_ref, next_ref)):
        value = acc_ref[0, k]
        for j in range(1, chains):
            value = value + acc_ref[j, k]
        ref[...] = value.astype(ref.dtype)


def collect(idx, got, per_part):
    members = got.shape[0]
    chains = 4
    piece = (members, SUB, LANE)
    return pl.pallas_call(
        functools.partial(collect_kernel, members, per_part, chains),
        out_shape=(
            jax.ShapeDtypeStruct(piece, jnp.bfloat16),
            jax.ShapeDtypeStruct(piece, jnp.float32),
            jax.ShapeDtypeStruct(piece, jnp.bfloat16),
            jax.ShapeDtypeStruct((SUB, LANE), jnp.float32),
        ),
        in_specs=[smem(), vmem()],
        out_specs=(vmem(),) * 4,
        scratch_shapes=[pltpu.VMEM((chains, 3) + piece, jnp.float32)],
        name="collect",
    )(idx, got)


def swap(x, axis):
    return lax.all_to_all(x, axis, 0, 0, tiled=True)


def per_device(features, weight, bias, cotangent, degree, tile_cols, edge_tile, edge_row, edge_col):
    rows, width = features.shape
    members = lax.axis_size("grp")
    rings = lax.axis_size("rep")
    listed = tile_cols.shape[1]
    per_part = listed // 3
    groups = rows // SUB
    half = lax.axis_index("grp") // groups
    contract = (((0,), (0,)), ((), ()))

    cut = features.reshape(groups, SUB, 2, LANE).transpose(0, 2, 1, 3)
    lane = lax.broadcasted_iota(jnp.int32, (groups, SUB, LANE), 2)
    names = jnp.pad(tile_cols[0], (0, LANE - listed))
    note = jnp.where(lane < LANE // 2, names[None, None, :], degree.reshape(groups, SUB, 1))
    sent = jnp.concatenate([cut, note.astype(jnp.bfloat16)[:, None]], axis=1)
    got = swap(jnp.concatenate([sent, sent], axis=0), "grp")
    nodes = jnp.concatenate([got[:, 0].reshape(-1, LANE), got[:, 1].reshape(-1, LANE)], axis=1)
    idx = got[:, 2, 0, :listed].astype(jnp.int32).reshape(-1)
    dinv_piece = lax.rsqrt(got[:, 2, :, LANE // 2].astype(jnp.float32)).reshape(-1, 1)

    weight_half = lax.dynamic_slice_in_dim(weight, half * LANE, LANE, 1)
    scaled = (jnp.dot(nodes, weight_half, preferred_element_type=jnp.float32) * dinv_piece).astype(jnp.bfloat16)
    scaled = scaled.reshape(members, SUB, LANE)
    from_left = shifted(scaled, "rep", 1)
    from_right = shifted(scaled, "rep", -1)

    tile = edge_tile[0]
    col = edge_col[0]
    key = (col // SUB) * (listed * SUB) + tile * SUB + col % SUB
    slab = build_slab(edge_row[0], key, rows, listed * rows)

    chosen = select(idx, from_left, scaled, from_right, per_part)
    window = swap(chosen.reshape(members, listed, SUB, LANE), "grp")
    dinv = lax.rsqrt(degree.astype(jnp.float32))[:, None]
    hidden, partial = layer(
        slab, window.reshape(2, listed * rows, LANE), dinv, bias[None, :], cotangent, listed
    )
    mine = swap(partial.reshape(members, listed + 1, SUB, LANE), "grp")
    previous_part, own_part, next_part, extra = collect(idx, mine, per_part)
    from_next = shifted(previous_part, "rep", -1)
    from_previous = shifted(next_part, "rep", 1)
    grad_sum = own_part + from_next.astype(jnp.float32) + from_previous.astype(jnp.float32)
    grad_piece = (grad_sum.reshape(-1, LANE) * dinv_piece).astype(jnp.bfloat16)
    local_weight = lax.dot_general(nodes, grad_piece, contract, preferred_element_type=jnp.float32)

    both = jnp.stack(
        [local_weight.reshape(members, SUB, LANE), grad_piece.astype(jnp.float32).reshape(members, SUB, LANE)], axis=1
    )
    both = swap(both, "grp")
    chunk = both[:, 0].reshape(2, groups, SUB, LANE).sum(axis=1)
    grad_scaled = both[:, 1].reshape(2, rows, LANE).transpose(1, 0, 2).reshape(rows, width).astype(jnp.bfloat16)
    grad_features = lax.dot_general(
        grad_scaled, weight, (((1,), (1,)), ((), ())), preferred_element_type=jnp.float32
    ).astype(jnp.bfloat16)

    share = jnp.concatenate([chunk, extra[None]], axis=0)
    share = swap(jnp.broadcast_to(share[None], (rings, 3, SUB, LANE)), "rep").sum(axis=0)
    bias_rows = share[2]
    grad_bias = jnp.concatenate([bias_rows[0] + bias_rows[2], bias_rows[1] + bias_rows[3]])
    whole = swap(jnp.broadcast_to(share[None, :2], (members, 2, SUB, LANE)), "grp")
    grad_weight = whole.transpose(0, 2, 1, 3).reshape(width, width)
    return (hidden, grad_features, grad_weight, grad_bias)


def solution(mesh):
    return jax.shard_map(
        per_device,
        mesh=mesh,
        in_specs=(
            P(("rep", "grp"), None),
            P(),
            P(),
            P(("rep", "grp"), None),
            P(("rep", "grp")),
            P(("rep", "grp"), None),
            P(("rep", "grp"), None),
            P(("rep", "grp"), None),
            P(("rep", "grp"), None),
        ),
        out_specs=(P(("rep", "grp"), None), P(("rep", "grp"), None), P(), P()),
        check_vma=False,
    )
```

```python
import functools

import jax
import jax.numpy as jnp
from jax import lax
from jax.experimental import pallas as pl
from jax.experimental.pallas import tpu as pltpu
from jax.sharding import PartitionSpec as P

SUB = 8
LANE = 128


def shifted(x, axis, by):
    size = lax.axis_size(axis)
    return lax.ppermute(x, axis, [(i, (i + by) % size) for i in range(size)])


def vmem():
    return pl.BlockSpec(memory_space=pltpu.VMEM)


def smem():
    return pl.BlockSpec(memory_space=pltpu.SMEM)


def count_kernel(chunk, xk_ref, yk_ref, own_ref, far_ref, acc_ref):
    edges = xk_ref.shape[1]
    tall = acc_ref.shape[0]
    wide = acc_ref.shape[1]
    for step in range(edges // chunk):
        xk = xk_ref[:, pl.ds(step * chunk, chunk)]
        yk = yk_ref[:, pl.ds(step * chunk, chunk)]
        left = (lax.broadcasted_iota(jnp.int32, (tall, chunk), 0) == xk).astype(jnp.float32).astype(jnp.bfloat16)
        right = (lax.broadcasted_iota(jnp.int32, (wide, chunk), 0) == yk).astype(jnp.float32).astype(jnp.bfloat16)
        part = lax.dot_general(left, right, (((1,), (1,)), ((), ())), preferred_element_type=jnp.float32)
        if step == 0:
            acc_ref[...] = part
        else:
            acc_ref[...] += part
    rows = own_ref.shape[0]
    first = own_ref.shape[1] // wide
    for block in range(tall // rows):
        out_ref, at = (own_ref, block) if block < first else (far_ref, block - first)
        out_ref[:, pl.ds(at * wide, wide)] = acc_ref[pl.ds(block * rows, rows), :].astype(jnp.bfloat16)


def build_slab(row, key, rows, keys):
    wide = 256
    edges = row.shape[0]
    chunk = 768 if edges % 768 == 0 else 128
    tall = rows * (keys // wide)
    xk = ((key // wide) * rows + row).reshape(1, edges)
    yk = (key % wide).reshape(1, edges)
    return pl.pallas_call(
        functools.partial(count_kernel, chunk),
        out_shape=(
            jax.ShapeDtypeStruct((rows, keys // 3), jnp.bfloat16),
            jax.ShapeDtypeStruct((rows, keys - keys // 3), jnp.bfloat16),
        ),
        in_specs=[vmem(), vmem()],
        out_specs=(vmem(), vmem()),
        scratch_shapes=[pltpu.VMEM((tall, wide), jnp.float32)],
        name="count",
    )(xk, yk)


def select_kernel(members, per_part, parts, idx_ref, *refs):
    sources, out_ref = refs[:-1], refs[-1]

    def one(d, carry):
        for number, part in enumerate(parts):
            for t in range(per_part):
                at = jnp.bitwise_and(idx_ref[d * 3 * per_part + part * per_part + t], members - 1)
                out_ref[d, number * per_part + t] = sources[number][at]
        return carry

    lax.fori_loop(0, members, one, 0)


def select(idx, parts, sources, per_part):
    members = sources[0].shape[0]
    return pl.pallas_call(
        functools.partial(select_kernel, members, per_part, parts),
        out_shape=jax.ShapeDtypeStruct((members, len(parts) * per_part, SUB, LANE), sources[0].dtype),
        in_specs=[smem()] + [vmem()] * len(sources),
        out_specs=vmem(),
        name="select",
    )(idx, *sources)


def store_partial(slab_ref, back, part_ref, half):
    groups = part_ref.shape[1]
    listed = slab_ref.shape[1] // (groups * SUB)
    span = listed * SUB
    partial = lax.dot_general(slab_ref[...], back, (((0,), (0,)), ((), ())), preferred_element_type=jnp.float32)
    for a in range(groups):
        piece = partial[a * span : (a + 1) * span, :].reshape(listed, SUB, LANE)
        part_ref[half, a, pl.ds(0, listed)] = piece.astype(jnp.bfloat16)


def layer_kernel(own_ref, far_ref, xown_ref, xfar_ref, dinv_ref, bias_ref, cot_ref, hid_ref, part_ref, back_ref, extra_ref):
    dinv = dinv_ref[...]
    sums = []
    for half in range(2):
        lanes = slice(half * LANE, (half + 1) * LANE)
        total = jnp.dot(own_ref[...], xown_ref[half], preferred_element_type=jnp.float32)
        total = total + jnp.dot(far_ref[...], xfar_ref[half], preferred_element_type=jnp.float32)
        pre = total * dinv + bias_ref[:, lanes]
        sig = jax.nn.sigmoid(pre)
        hid_ref[:, lanes] = (pre * sig).astype(hid_ref.dtype)
        grad_pre = cot_ref[:, lanes].astype(jnp.float32) * sig * (1.0 + pre * (1.0 - sig))
        sums.append(jnp.sum(grad_pre, axis=0, keepdims=True))
        back = (grad_pre * dinv).astype(jnp.bfloat16)
        back_ref[:, lanes] = back
        store_partial(far_ref, back, part_ref, half)
    high = [s.astype(jnp.bfloat16).astype(jnp.float32) for s in sums]
    low = [s - h for s, h in zip(sums, high)]
    at = lax.broadcasted_iota(jnp.int32, (SUB, LANE), 0)
    extra = jnp.zeros((SUB, LANE), jnp.float32)
    for index, value in enumerate(high + low):
        extra = jnp.where(at == index, value, extra)
    extra_ref[...] = extra


def layer(own, far, xown, xfar, dinv, bias, cotangent, listed):
    rows, width = cotangent.shape
    groups = rows // SUB
    return pl.pallas_call(
        layer_kernel,
        out_shape=(
            jax.ShapeDtypeStruct((rows, width), jnp.bfloat16),
            jax.ShapeDtypeStruct((2, groups, listed - listed // 3, SUB, LANE), jnp.bfloat16),
            jax.ShapeDtypeStruct((rows, width), jnp.bfloat16),
            jax.ShapeDtypeStruct((SUB, LANE), jnp.float32),
        ),
        in_specs=[vmem()] * 7,
        out_specs=(vmem(),) * 4,
        name="layer",
    )(own, far, xown, xfar, dinv, bias, cotangent)


def own_kernel(own_ref, back_ref, extra_ref, part_ref):
    groups = part_ref.shape[1]
    last = part_ref.shape[2] - 1
    extra = extra_ref[...].astype(jnp.bfloat16)
    for half in range(2):
        store_partial(own_ref, back_ref[:, half * LANE : (half + 1) * LANE], part_ref, half)
        for a in range(groups):
            part_ref[half, a, last] = extra


def own_partial(own, back, extra):
    groups = back.shape[0] // SUB
    listed = own.shape[1] // (groups * SUB)
    return pl.pallas_call(
        own_kernel,
        out_shape=jax.ShapeDtypeStruct((2, groups, listed + 1, SUB, LANE), jnp.bfloat16),
        in_specs=[vmem()] * 3,
        out_specs=vmem(),
        name="own",
    )(own, back, extra)


def collect_kernel(members, per_part, parts, chains, idx_ref, got_ref, *refs):
    acc_ref = refs[-1]
    outs = refs[: len(parts)]
    more = len(refs) - 1 - len(parts)
    acc_ref[...] = jnp.zeros_like(acc_ref)

    def some(step, extra):
        for number, part in enumerate(parts):
            for t in range(per_part):
                for j in range(chains):
                    d = step * chains + j
                    at = jnp.bitwise_and(idx_ref[d * 3 * per_part + part * per_part + t], members - 1)
                    acc_ref[j, number, at] += got_ref[d, number * per_part + t].astype(jnp.float32)
        if more:
            for j in range(chains):
                extra = extra + got_ref[step * chains + j, len(parts) * per_part].astype(jnp.float32)
        return extra

    extra = lax.fori_loop(0, members // chains, some, jnp.zeros((SUB, LANE), jnp.float32))
    if more:
        refs[len(parts)][...] = extra
    for number, ref in enumerate(outs):
        value = acc_ref[0, number]
        for j in range(1, chains):
            value = value + acc_ref[j, number]
        ref[...] = value.astype(ref.dtype)


def collect(idx, parts, got, per_part, dtype):
    members = got.shape[0]
    chains = 4
    piece = (members, SUB, LANE)
    outs = [jax.ShapeDtypeStruct(piece, dtype) for _ in parts]
    if got.shape[1] > len(parts) * per_part:
        outs.append(jax.ShapeDtypeStruct((SUB, LANE), jnp.float32))
    return pl.pallas_call(
        functools.partial(collect_kernel, members, per_part, parts, chains),
        out_shape=tuple(outs),
        in_specs=[smem(), vmem()],
        out_specs=(vmem(),) * len(outs),
        scratch_shapes=[pltpu.VMEM((chains, len(parts)) + piece, jnp.float32)],
        name="collect",
    )(idx, got)


def swap(x, axis):
    return lax.all_to_all(x, axis, 0, 0, tiled=True)


def per_device(features, weight, bias, cotangent, degree, tile_cols, edge_tile, edge_row, edge_col):
    rows, width = features.shape
    members = lax.axis_size("grp")
    rings = lax.axis_size("rep")
    listed = tile_cols.shape[1]
    per_part = listed // 3
    groups = rows // SUB
    half = lax.axis_index("grp") // groups
    contract = (((0,), (0,)), ((), ()))

    cut = features.reshape(groups, SUB, 2, LANE).transpose(0, 2, 1, 3)
    lane = lax.broadcasted_iota(jnp.int32, (groups, SUB, LANE), 2)
    names = jnp.pad(tile_cols[0], (0, LANE - listed))
    note = jnp.where(lane < LANE // 2, names[None, None, :], degree.reshape(groups, SUB, 1))
    sent = jnp.concatenate([cut, note.astype(jnp.bfloat16)[:, None]], axis=1)
    got = swap(jnp.concatenate([sent, sent], axis=0), "grp")
    nodes = jnp.concatenate([got[:, 0].reshape(-1, LANE), got[:, 1].reshape(-1, LANE)], axis=1)
    idx = got[:, 2, 0, :listed].astype(jnp.int32).reshape(-1)
    dinv_piece = lax.rsqrt(got[:, 2, :, LANE // 2].astype(jnp.float32)).reshape(-1, 1)

    weight_half = lax.dynamic_slice_in_dim(weight, half * LANE, LANE, 1)
    scaled = (jnp.dot(nodes, weight_half, preferred_element_type=jnp.float32) * dinv_piece).astype(jnp.bfloat16)
    scaled = scaled.reshape(members, SUB, LANE)
    from_left = shifted(scaled, "rep", 1)
    from_right = shifted(scaled, "rep", -1)

    tile = edge_tile[0]
    col = edge_col[0]
    far_tile = jnp.where(tile < per_part, tile, tile - per_part)
    is_own = (tile >= per_part) & (tile < 2 * per_part)
    own_key = (col // SUB) * (per_part * SUB) + (tile - per_part) * SUB
    far_key = per_part * rows + (col // SUB) * (2 * per_part * SUB) + far_tile * SUB
    key = jnp.where(is_own, own_key, far_key) + col % SUB
    slab_own, slab_far = build_slab(edge_row[0], key, rows, listed * rows)

    chosen_own = select(idx, (1,), (scaled,), per_part)
    window_own = swap(chosen_own, "grp")
    chosen_far = select(idx, (0, 2), (from_left, from_right), per_part)
    window_far = swap(chosen_far, "grp")
    dinv = lax.rsqrt(degree.astype(jnp.float32))[:, None]
    hidden, partial_far, back, extra = layer(
        slab_own,
        slab_far,
        window_own.reshape(2, per_part * rows, LANE),
        window_far.reshape(2, 2 * per_part * rows, LANE),
        dinv,
        bias[None, :],
        cotangent,
        listed,
    )
    mine_far = swap(partial_far.reshape(members, 2 * per_part, SUB, LANE), "grp")
    partial_own = own_partial(slab_own, back, extra)
    mine_own = swap(partial_own.reshape(members, per_part + 1, SUB, LANE), "grp")
    previous_part, next_part = collect(idx, (0, 2), mine_far, per_part, jnp.bfloat16)
    from_next = shifted(previous_part, "rep", -1)
    from_previous = shifted(next_part, "rep", 1)
    own_part, extra = collect(idx, (1,), mine_own, per_part, jnp.float32)
    grad_sum = own_part + from_next.astype(jnp.float32) + from_previous.astype(jnp.float32)
    grad_piece = (grad_sum.reshape(-1, LANE) * dinv_piece).astype(jnp.bfloat16)
    local_weight = lax.dot_general(nodes, grad_piece, contract, preferred_element_type=jnp.float32)

    both = jnp.stack(
        [local_weight.astype(jnp.bfloat16).reshape(members, SUB, LANE), grad_piece.reshape(members, SUB, LANE)], axis=1
    )
    both = swap(both, "grp")
    chunk = both[:, 0].reshape(2, groups, SUB, LANE).astype(jnp.float32).sum(axis=1)
    grad_scaled = both[:, 1].reshape(2, rows, LANE).transpose(1, 0, 2).reshape(rows, width)
    grad_features = lax.dot_general(
        grad_scaled, weight, (((1,), (1,)), ((), ())), preferred_element_type=jnp.float32
    ).astype(jnp.bfloat16)

    share = jnp.concatenate([chunk, extra[None]], axis=0)
    share = swap(jnp.broadcast_to(share[None], (rings, 3, SUB, LANE)), "rep").sum(axis=0)
    bias_rows = share[2]
    grad_bias = jnp.concatenate([bias_rows[0] + bias_rows[2], bias_rows[1] + bias_rows[3]])
    final = share[None, :2].astype(jnp.bfloat16)
    whole = swap(jnp.broadcast_to(final, (members, 2, SUB, LANE)), "grp")
    grad_weight = whole.transpose(0, 2, 1, 3).reshape(width, width).astype(jnp.float32)
    return (hidden, grad_features, grad_weight, grad_bias)


def solution(mesh):
    return jax.shard_map(
        per_device,
        mesh=mesh,
        in_specs=(
            P(("rep", "grp"), None),
            P(),
            P(),
            P(("rep", "grp"), None),
            P(("rep", "grp")),
            P(("rep", "grp"), None),
            P(("rep", "grp"), None),
            P(("rep", "grp"), None),
            P(("rep", "grp"), None),
        ),
        out_specs=(P(("rep", "grp"), None), P(("rep", "grp"), None), P(), P()),
        check_vma=False,
    )
```

```python
import functools

import jax
import jax.numpy as jnp
from jax import lax
from jax.experimental import pallas as pl
from jax.experimental.pallas import tpu as pltpu
from jax.sharding import PartitionSpec as P


SUB = 8
LANE = 128


def shifted(x, axis, by):
    size = lax.axis_size(axis)
    return lax.ppermute(x, axis, [(i, (i + by) % size) for i in range(size)])


def vmem():
    return pl.BlockSpec(memory_space=pltpu.VMEM)


def smem():
    return pl.BlockSpec(memory_space=pltpu.SMEM)


def count_kernel(chunk, xk_ref, yk_ref, out_ref, acc_ref):
    edges = xk_ref.shape[1]
    tall = acc_ref.shape[0]
    wide = acc_ref.shape[1]
    for step in range(edges // chunk):
        xk = xk_ref[:, pl.ds(step * chunk, chunk)]
        yk = yk_ref[:, pl.ds(step * chunk, chunk)]
        left = (lax.broadcasted_iota(jnp.int32, (tall, chunk), 0) == xk).astype(jnp.float32).astype(jnp.bfloat16)
        right = (lax.broadcasted_iota(jnp.int32, (wide, chunk), 0) == yk).astype(jnp.float32).astype(jnp.bfloat16)
        part = lax.dot_general(left, right, (((1,), (1,)), ((), ())), preferred_element_type=jnp.float32)
        if step == 0:
            acc_ref[...] = part
        else:
            acc_ref[...] += part
    rows = out_ref.shape[0]
    for block in range(tall // rows):
        out_ref[:, pl.ds(block * wide, wide)] = acc_ref[pl.ds(block * rows, rows), :].astype(jnp.bfloat16)


def build_slab(row, key, rows, keys):
    wide = 256
    edges = row.shape[0]
    chunk = 768 if edges % 768 == 0 else 128
    tall = rows * (keys // wide)
    xk = ((key // wide) * rows + row).reshape(1, edges)
    yk = (key % wide).reshape(1, edges)
    return pl.pallas_call(
        functools.partial(count_kernel, chunk),
        out_shape=jax.ShapeDtypeStruct((rows, keys), jnp.bfloat16),
        in_specs=[vmem(), vmem()],
        out_specs=vmem(),
        scratch_shapes=[pltpu.VMEM((tall, wide), jnp.float32)],
        name="count",
    )(xk, yk)


def select_kernel(members, per_part, idx_ref, a_ref, b_ref, c_ref, out_ref):
    listed = 3 * per_part

    def one(d, carry):
        base = d * listed
        for t in range(listed):
            src = (a_ref, b_ref, c_ref)[t // per_part]
            at = jnp.bitwise_and(idx_ref[base + t], members - 1)
            out_ref[base + t] = src[at]
        return carry

    lax.fori_loop(0, members, one, 0)


def select(idx, left, own, right, per_part):
    members = own.shape[0]
    return pl.pallas_call(
        functools.partial(select_kernel, members, per_part),
        out_shape=jax.ShapeDtypeStruct((members * 3 * per_part, SUB, LANE), own.dtype),
        in_specs=[smem(), vmem(), vmem(), vmem()],
        out_specs=vmem(),
        name="select",
    )(idx, left, own, right)


def layer_kernel(listed, slab_ref, x_ref, weight_ref, dinv_ref, bias_ref, cot_ref, hid_ref, part_ref):
    dinv = dinv_ref[...]
    groups = part_ref.shape[1]
    span = listed * SUB
    rows = [jnp.dot(slab_ref[...], x_ref[half], preferred_element_type=jnp.float32) for half in range(2)]
    gathered = jnp.concatenate(rows, axis=1)
    high = gathered.astype(jnp.bfloat16)
    low = (gathered - high.astype(jnp.float32)).astype(jnp.bfloat16)
    weight = weight_ref[...]
    total = jnp.dot(high, weight, preferred_element_type=jnp.float32)
    total = total + jnp.dot(low, weight, preferred_element_type=jnp.float32)
    pre = total * dinv + bias_ref[...]
    sig = jax.nn.sigmoid(pre)
    hid_ref[...] = (pre * sig).astype(hid_ref.dtype)
    grad_pre = cot_ref[...].astype(jnp.float32) * sig * (1.0 + pre * (1.0 - sig))
    back = (grad_pre * dinv).astype(jnp.bfloat16)
    contract = (((0,), (0,)), ((), ()))
    grad = lax.dot_general(high, back, contract, preferred_element_type=jnp.float32)
    grad = grad + lax.dot_general(low, back, contract, preferred_element_type=jnp.float32)
    sums = jnp.sum(grad_pre, axis=0, keepdims=True)
    sums_high = sums.astype(jnp.bfloat16).astype(jnp.float32)
    sums_low = sums - sums_high
    at = lax.broadcasted_iota(jnp.int32, (SUB, LANE), 0)
    extra = jnp.zeros((SUB, LANE), jnp.float32)
    for index, value in enumerate((sums_high, sums_low)):
        for half in range(2):
            lanes = slice(half * LANE, (half + 1) * LANE)
            extra = jnp.where(at == 2 * index + half, value[:, lanes], extra)
    extra = extra.astype(jnp.bfloat16)
    for half in range(2):
        lanes = slice(half * LANE, (half + 1) * LANE)
        partial = lax.dot_general(slab_ref[...], back[:, lanes], contract, preferred_element_type=jnp.float32)
        for a in range(groups):
            piece = partial[a * span : (a + 1) * span, :].reshape(listed, SUB, LANE)
            part_ref[half, a, pl.ds(0, listed)] = piece.astype(jnp.bfloat16)
            part_ref[half, a, listed] = extra
            top = (half * groups + a) * SUB
            for other in range(2):
                block = grad[top : top + SUB, other * LANE : (other + 1) * LANE]
                part_ref[half, a, listed + 1 + other] = block.astype(jnp.bfloat16)


def layer(slab, x, weight, dinv, bias, cotangent, listed):
    rows, width = cotangent.shape
    groups = rows // SUB
    return pl.pallas_call(
        functools.partial(layer_kernel, listed),
        out_shape=(
            jax.ShapeDtypeStruct((rows, width), jnp.bfloat16),
            jax.ShapeDtypeStruct((2, groups, listed + 3, SUB, LANE), jnp.bfloat16),
        ),
        in_specs=[vmem()] * 6,
        out_specs=(vmem(), vmem()),
        name="layer",
    )(slab, x, weight, dinv, bias, cotangent)


def collect_kernel(members, per_part, chains, idx_ref, got_ref, prev_ref, own_ref, next_ref, acc_ref):
    listed = 3 * per_part
    acc_ref[...] = jnp.zeros_like(acc_ref)

    def some(step, carry):
        for t in range(listed):
            for j in range(chains):
                d = step * chains + j
                at = jnp.bitwise_and(idx_ref[d * listed + t], members - 1)
                acc_ref[j, t // per_part, at] += got_ref[d, t].astype(jnp.float32)
        return carry

    lax.fori_loop(0, members // chains, some, 0)
    for k, ref in enumerate((prev_ref, own_ref, next_ref)):
        value = acc_ref[0, k]
        for j in range(1, chains):
            value = value + acc_ref[j, k]
        ref[...] = value.astype(ref.dtype)


def collect(idx, got, per_part):
    members = got.shape[0]
    chains = 4
    piece = (members, SUB, LANE)
    return pl.pallas_call(
        functools.partial(collect_kernel, members, per_part, chains),
        out_shape=(
            jax.ShapeDtypeStruct(piece, jnp.bfloat16),
            jax.ShapeDtypeStruct(piece, jnp.float32),
            jax.ShapeDtypeStruct(piece, jnp.bfloat16),
        ),
        in_specs=[smem(), vmem()],
        out_specs=(vmem(),) * 3,
        scratch_shapes=[pltpu.VMEM((chains, 3) + piece, jnp.float32)],
        name="collect",
    )(idx, got)


def swap(x, axis):
    return lax.all_to_all(x, axis, 0, 0, tiled=True)


def per_device(features, weight, bias, cotangent, degree, tile_cols, edge_tile, edge_row, edge_col):
    rows, width = features.shape
    members = lax.axis_size("grp")
    rings = lax.axis_size("rep")
    listed = tile_cols.shape[1]
    per_part = listed // 3
    groups = rows // SUB
    dinv = lax.rsqrt(degree.astype(jnp.float32))[:, None]

    scaled = (features.astype(jnp.float32) * dinv).astype(jnp.bfloat16)
    cut = scaled.reshape(groups, SUB, 2, LANE).transpose(2, 0, 1, 3).reshape(members, SUB, LANE)
    lane = lax.broadcasted_iota(jnp.int32, (groups, SUB, LANE), 2)
    names = jnp.pad(tile_cols[0], (0, LANE - listed))
    note = jnp.where(lane < LANE // 2, names[None, None, :], degree.reshape(groups, SUB, 1)).astype(jnp.bfloat16)
    got = swap(jnp.stack([cut, jnp.concatenate([note, note], axis=0)], axis=1), "grp")
    own = got[:, 0]
    idx = got[:, 1, 0, :listed].astype(jnp.int32).reshape(-1)
    dinv_piece = lax.rsqrt(got[:, 1, :, LANE // 2].astype(jnp.float32))[:, :, None]
    from_left = shifted(own, "rep", 1)
    from_right = shifted(own, "rep", -1)

    tile = edge_tile[0]
    col = edge_col[0]
    key = (col // SUB) * (listed * SUB) + tile * SUB + col % SUB
    slab = build_slab(edge_row[0], key, rows, listed * rows)

    chosen = select(idx, from_left, own, from_right, per_part)
    window = swap(chosen.reshape(members, listed, SUB, LANE), "grp")
    hidden, partial = layer(
        slab, window.reshape(2, listed * rows, LANE), weight, dinv, bias[None, :], cotangent, listed
    )
    mine = swap(partial.reshape(members, listed + 3, SUB, LANE), "grp")

    share = mine[:, listed:].astype(jnp.float32).sum(axis=0)
    share = swap(jnp.broadcast_to(share[None], (rings, 3, SUB, LANE)), "rep")
    share = share.sum(axis=0)
    grad_bias = jnp.concatenate([share[0, 0] + share[0, 2], share[0, 1] + share[0, 3]])

    previous_part, own_part, next_part = collect(idx, mine, per_part)
    from_next = shifted(previous_part, "rep", -1)
    from_previous = shifted(next_part, "rep", 1)
    grad_sum = own_part + from_next.astype(jnp.float32) + from_previous.astype(jnp.float32)
    grad_piece = (grad_sum * dinv_piece).astype(jnp.bfloat16)
    final = jnp.broadcast_to(share[None, 1:].astype(jnp.bfloat16), (members, 2, SUB, LANE))
    final = swap(jnp.concatenate([grad_piece[:, None], final], axis=1), "grp")
    grad_scaled = final[:, 0].reshape(2, rows, LANE).transpose(1, 0, 2).reshape(rows, width)
    grad_features = lax.dot_general(
        grad_scaled, weight, (((1,), (1,)), ((), ())), preferred_element_type=jnp.float32
    ).astype(jnp.bfloat16)
    grad_weight = final[:, 1:].transpose(0, 2, 1, 3).reshape(width, width).astype(jnp.float32)
    return (hidden, grad_features, grad_weight, grad_bias)


def solution(mesh):
    return jax.shard_map(
        per_device,
        mesh=mesh,
        in_specs=(
            P(("rep", "grp"), None),
            P(),
            P(),
            P(("rep", "grp"), None),
            P(("rep", "grp")),
            P(("rep", "grp"), None),
            P(("rep", "grp"), None),
            P(("rep", "grp"), None),
            P(("rep", "grp"), None),
        ),
        out_specs=(P(("rep", "grp"), None), P(("rep", "grp"), None), P(), P()),
        check_vma=False,
    )
```

```python
import functools

import jax
import jax.numpy as jnp
from jax import lax
from jax.experimental import pallas as pl
from jax.experimental.pallas import tpu as pltpu
from jax.sharding import PartitionSpec as P


SUB = 8
LANE = 128
MIB = 1 << 20


def with_partner(x, axis):
    return lax.ppermute(x, axis, [(i, i ^ 1) for i in range(lax.axis_size(axis))])


def with_other(x, axis):
    size = lax.axis_size(axis)
    return lax.ppermute(x, axis, [(i, (i + 1 if i % 2 else i - 1) % size) for i in range(size)])


def vmem():
    return pl.BlockSpec(memory_space=pltpu.VMEM)


def smem():
    return pl.BlockSpec(memory_space=pltpu.SMEM)


def hbm():
    return pl.BlockSpec(memory_space=pltpu.HBM)


def call(kernel, mib, out_shape, in_specs, out_specs, scratch=()):
    return pl.pallas_call(
        kernel,
        out_shape=out_shape,
        in_specs=in_specs,
        out_specs=out_specs,
        scratch_shapes=list(scratch),
        compiler_params=pltpu.CompilerParams(vmem_limit_bytes=mib * MIB),
    )


def cut_kernel(x_ref, degree_ref, cols_ref, out_ref, dinv_ref, names_ref):
    rows = x_ref.shape[0]
    groups = rows // SUB
    square = (rows, rows)
    diagonal = lax.broadcasted_iota(jnp.int32, square, 0) == lax.broadcasted_iota(jnp.int32, square, 1)
    degree = jnp.sum(jnp.where(diagonal, degree_ref[...].astype(jnp.float32), 0.0), axis=1, keepdims=True)
    dinv = lax.rsqrt(degree)
    dinv_ref[...] = dinv
    names_ref[...] = jnp.zeros_like(names_ref)
    names_ref[:, pl.ds(0, cols_ref.shape[1])] = cols_ref[...].astype(jnp.float32)
    lane = lax.broadcasted_iota(jnp.int32, (rows, LANE), 1)
    note = jnp.where(lane < LANE // 2, names_ref[...], degree).reshape(groups, SUB, LANE).astype(jnp.bfloat16)
    for half in range(2):
        scaled = x_ref[:, half * LANE : (half + 1) * LANE].astype(jnp.float32) * dinv
        scaled = scaled.reshape(groups, SUB, LANE).astype(jnp.bfloat16)
        for a in range(groups):
            out_ref[half * groups + a, 0] = scaled[a]
            out_ref[half * groups + a, 1] = note[a]


def cut(features, degree, cols):
    rows = features.shape[0]
    return call(
        cut_kernel,
        60,
        (
            jax.ShapeDtypeStruct((2 * rows // SUB, 2, SUB, LANE), jnp.bfloat16),
            jax.ShapeDtypeStruct((rows, 1), jnp.float32),
        ),
        [vmem()] * 3,
        (vmem(), vmem()),
        [pltpu.VMEM((1, LANE), jnp.float32)],
    )(features, degree, cols)


def count_kernel(chunk, xk_ref, yk_ref, out_ref, acc_ref):
    edges = xk_ref.shape[1]
    tall = acc_ref.shape[0]
    wide = acc_ref.shape[1]
    for step in range(edges // chunk):
        xk = xk_ref[:, pl.ds(step * chunk, chunk)]
        yk = yk_ref[:, pl.ds(step * chunk, chunk)]
        left = (lax.broadcasted_iota(jnp.int32, (tall, chunk), 0) == xk).astype(jnp.float32).astype(jnp.bfloat16)
        right = (lax.broadcasted_iota(jnp.int32, (wide, chunk), 0) == yk).astype(jnp.float32).astype(jnp.bfloat16)
        part = lax.dot_general(left, right, (((1,), (1,)), ((), ())), preferred_element_type=jnp.float32)
        if step == 0:
            acc_ref[...] = part
        else:
            acc_ref[...] += part
    rows = out_ref.shape[0]
    for block in range(tall // rows):
        out_ref[:, pl.ds(block * wide, wide)] = acc_ref[pl.ds(block * rows, rows), :].astype(jnp.bfloat16)


def build_slab(row, key, rows, keys):
    wide = 256
    edges = row.shape[0]
    chunk = 768 if edges % 768 == 0 else 128
    tall = rows * (keys // wide)
    xk = ((key // wide) * rows + row).reshape(1, edges)
    yk = (key % wide).reshape(1, edges)
    return pl.pallas_call(
        functools.partial(count_kernel, chunk),
        out_shape=jax.ShapeDtypeStruct((rows, keys), jnp.bfloat16),
        in_specs=[vmem(), vmem()],
        out_specs=vmem(),
        scratch_shapes=[pltpu.VMEM((tall, wide), jnp.float32)],
        compiler_params=pltpu.CompilerParams(vmem_limit_bytes=24 * MIB),
        name="count",
    )(xk, yk)


def select_kernel(members, per_part, idx_ref, first_ref, own_ref, second_ref, out_ref, near_ref, made_ref, sems):
    listed = 3 * per_part
    near_ref[pl.ds(0, members)] = first_ref[...]
    near_ref[pl.ds(members, members)] = second_ref[...]
    steps = sems.shape[0]
    span = members // steps

    def one(d, carry):
        for t in range(listed):
            at = idx_ref[d * listed + t]
            if t // per_part == 1:
                made_ref[d, t] = own_ref[jnp.bitwise_and(at, members - 1)]
            else:
                made_ref[d, t] = near_ref[jnp.bitwise_and(at, 2 * members - 1)]
        return carry

    copies = []
    for step in range(steps):
        lax.fori_loop(step * span, (step + 1) * span, one, 0)
        part = pl.ds(step * span, span)
        copies.append(pltpu.make_async_copy(made_ref.at[part], out_ref.at[part], sems.at[step]))
        copies[-1].start()
    for copy in copies:
        copy.wait()


def select(idx, first, own, second, per_part):
    members = own.shape[0]
    shape = (members, 3 * per_part, SUB, LANE)
    return call(
        functools.partial(select_kernel, members, per_part),
        6,
        jax.ShapeDtypeStruct(shape, own.dtype),
        [smem()] + [vmem()] * 3,
        hbm(),
        [
            pltpu.VMEM((2 * members, SUB, LANE), own.dtype),
            pltpu.VMEM(shape, own.dtype),
            pltpu.SemaphoreType.DMA((4,)),
        ],
    )(idx, first, own, second)


def layer_kernel(listed, slab_ref, x_ref, weight_ref, dinv_ref, bias_ref, cot_ref, hid_ref, out_ref, part_ref, sems):
    dinv = dinv_ref[...]
    groups = part_ref.shape[1]
    span = listed * SUB
    rows = [jnp.dot(slab_ref[...], x_ref[half], preferred_element_type=jnp.float32) for half in range(2)]
    gathered = jnp.concatenate(rows, axis=1)
    high = gathered.astype(jnp.bfloat16)
    low = (gathered - high.astype(jnp.float32)).astype(jnp.bfloat16)
    weight = weight_ref[...]
    total = jnp.dot(high, weight, preferred_element_type=jnp.float32)
    total = total + jnp.dot(low, weight, preferred_element_type=jnp.float32)
    pre = total * dinv + bias_ref[...]
    sig = jax.nn.sigmoid(pre)
    hid_ref[...] = (pre * sig).astype(hid_ref.dtype)
    grad_pre = cot_ref[...].astype(jnp.float32) * sig * (1.0 + pre * (1.0 - sig))
    back = (grad_pre * dinv).astype(jnp.bfloat16)
    contract = (((0,), (0,)), ((), ()))
    grad = lax.dot_general(high, back, contract, preferred_element_type=jnp.float32)
    grad = grad + lax.dot_general(low, back, contract, preferred_element_type=jnp.float32)
    sums = jnp.sum(grad_pre, axis=0, keepdims=True)
    sums_high = sums.astype(jnp.bfloat16).astype(jnp.float32)
    sums_low = sums - sums_high
    at = lax.broadcasted_iota(jnp.int32, (SUB, LANE), 0)
    extra = jnp.zeros((SUB, LANE), jnp.float32)
    for index, value in enumerate((sums_high, sums_low)):
        for half in range(2):
            lanes = slice(half * LANE, (half + 1) * LANE)
            extra = jnp.where(at == 2 * index + half, value[:, lanes], extra)
    extra = extra.astype(jnp.bfloat16)
    copies = []
    for half in range(2):
        lanes = slice(half * LANE, (half + 1) * LANE)
        partial = lax.dot_general(slab_ref[...], back[:, lanes], contract, preferred_element_type=jnp.float32)
        for a in range(groups):
            piece = partial[a * span : (a + 1) * span, :].reshape(listed, SUB, LANE)
            part_ref[half, a, pl.ds(0, listed)] = piece.astype(jnp.bfloat16)
            part_ref[half, a, listed] = extra
            top = (half * groups + a) * SUB
            for other in range(2):
                block = grad[top : top + SUB, other * LANE : (other + 1) * LANE]
                part_ref[half, a, listed + 1 + other] = block.astype(jnp.bfloat16)
        copies.append(pltpu.make_async_copy(part_ref.at[half], out_ref.at[half], sems.at[half]))
        copies[-1].start()
    for copy in copies:
        copy.wait()


def layer(slab, x, weight, dinv, bias, cotangent, listed):
    rows, width = cotangent.shape
    shape = (2, rows // SUB, listed + 3, SUB, LANE)
    return call(
        functools.partial(layer_kernel, listed),
        16,
        (jax.ShapeDtypeStruct((rows, width), jnp.bfloat16), jax.ShapeDtypeStruct(shape, jnp.bfloat16)),
        [vmem()] * 6,
        (vmem(), hbm()),
        [pltpu.VMEM(shape, jnp.bfloat16), pltpu.SemaphoreType.DMA((2,))],
    )(slab, x, weight, dinv, bias, cotangent)


def collect_kernel(members, per_part, parts, chains, idx_ref, got_ref, *refs):
    outs, acc_ref = refs[:-1], refs[-1]
    acc_ref[...] = jnp.zeros_like(acc_ref)
    tiles = acc_ref.shape[1]

    def some(step, carry):
        for part in parts:
            for t in range(part * per_part, (part + 1) * per_part):
                for j in range(chains):
                    d = step * chains + j
                    at = jnp.bitwise_and(idx_ref[d * 3 * per_part + t], tiles - 1)
                    acc_ref[j, at] += got_ref[d, t].astype(jnp.float32)
        return carry

    lax.fori_loop(0, members // chains, some, 0)
    for number, ref in enumerate(outs):
        part = pl.ds(number * members, members)
        value = acc_ref[0, part]
        for j in range(1, chains):
            value = value + acc_ref[j, part]
        ref[...] = value.astype(ref.dtype)


def collect(idx, parts, got, per_part, dtype):
    members = got.shape[0]
    chains = 4
    piece = (members, SUB, LANE)
    return call(
        functools.partial(collect_kernel, members, per_part, parts, chains),
        6,
        tuple(jax.ShapeDtypeStruct(piece, dtype) for _ in parts),
        [smem(), vmem()],
        (vmem(),) * len(parts),
        [pltpu.VMEM((chains, len(parts) * members, SUB, LANE), jnp.float32)],
    )(idx, got)


def join_kernel(got_ref, own_ref, first_ref, second_ref, share_ref, out_ref, bias_ref):
    members = own_ref.shape[0]
    total = share_ref[0]
    for ring in range(1, share_ref.shape[0]):
        total = total + share_ref[ring]
    for half in range(2):
        bias_ref[:, half * LANE : (half + 1) * LANE] = total[0, half : half + 1] + total[0, half + 2 : half + 3]
    rows = [total[1].astype(jnp.bfloat16), total[2].astype(jnp.bfloat16)]
    for m in range(members):
        dinv = lax.rsqrt(got_ref[m, 1].astype(jnp.float32)[:, LANE // 2 : LANE // 2 + 1])
        grad = own_ref[m] + first_ref[m].astype(jnp.float32) + second_ref[m].astype(jnp.float32)
        out_ref[m, 0] = (grad * dinv).astype(jnp.bfloat16)
        out_ref[m, 1] = rows[0]
        out_ref[m, 2] = rows[1]


def join(got, own, first, second, share):
    members = own.shape[0]
    return call(
        join_kernel,
        4,
        (
            jax.ShapeDtypeStruct((members, 3, SUB, LANE), jnp.bfloat16),
            jax.ShapeDtypeStruct((1, 2 * LANE), jnp.float32),
        ),
        [vmem()] * 5,
        (vmem(), vmem()),
    )(got, own, first, second, share)


def swap(x, axis):
    return lax.all_to_all(x, axis, 0, 0, tiled=True)


def per_device(features, weight, bias, cotangent, degree, tile_cols, edge_tile, edge_row, edge_col):
    rows, width = features.shape
    members = lax.axis_size("grp")
    rings = lax.axis_size("rep")
    listed = tile_cols.shape[1]
    per_part = listed // 3

    payload, dinv = cut(features, degree[None, :], tile_cols)
    got = swap(payload, "grp")
    own = got[:, 0]
    first = with_partner(own, "rep")
    second = with_other(own, "rep")

    names = got[:, 1, 0, :listed].astype(jnp.int32)
    part = lax.broadcasted_iota(jnp.int32, names.shape, 1) // per_part
    even = lax.axis_index("rep") % 2 == 0
    late = jnp.where(even, part == 0, part == 2)
    idx = (names % members + jnp.where(late, members, 0)).reshape(-1)

    tile = edge_tile[0]
    col = edge_col[0]
    key = (col // SUB) * (listed * SUB) + tile * SUB + col % SUB
    slab = build_slab(edge_row[0], key, rows, listed * rows)

    window = swap(select(idx, first, own, second, per_part), "grp")
    hidden, partial = layer(
        slab, window.reshape(2, listed * rows, LANE), weight, dinv, bias[None, :], cotangent, listed
    )
    mine = swap(partial.reshape(members, listed + 3, SUB, LANE), "grp")

    share = mine[:, listed:].astype(jnp.float32).sum(axis=0)
    share = swap(jnp.broadcast_to(share[None], (rings, 3, SUB, LANE)), "rep")
    to_first, to_second = collect(idx, (0, 2), mine, per_part, jnp.bfloat16)
    from_first = with_partner(to_first, "rep")
    from_second = with_other(to_second, "rep")
    (own_sum,) = collect(idx, (1,), mine, per_part, jnp.float32)

    final, grad_bias = join(got, own_sum, from_first, from_second, share)
    final = swap(final, "grp")
    grad_scaled = final[:, 0].reshape(2, rows, LANE).transpose(1, 0, 2).reshape(rows, width)
    grad_features = lax.dot_general(
        grad_scaled, weight, (((1,), (1,)), ((), ())), preferred_element_type=jnp.float32
    ).astype(jnp.bfloat16)
    grad_weight = final[:, 1:].transpose(0, 2, 1, 3).reshape(width, width).astype(jnp.float32)
    return (hidden, grad_features, grad_weight, grad_bias[0])


def solution(mesh):
    return jax.shard_map(
        per_device,
        mesh=mesh,
        in_specs=(
            P(("rep", "grp"), None),
            P(),
            P(),
            P(("rep", "grp"), None),
            P(("rep", "grp")),
            P(("rep", "grp"), None),
            P(("rep", "grp"), None),
            P(("rep", "grp"), None),
            P(("rep", "grp"), None),
        ),
        out_specs=(P(("rep", "grp"), None), P(("rep", "grp"), None), P(), P()),
        check_vma=False,
    )
```

```python
import functools

import jax
import jax.numpy as jnp
from jax import lax
from jax.experimental import pallas as pl
from jax.experimental.pallas import tpu as pltpu
from jax.sharding import PartitionSpec as P


SUB = 8
LANE = 128
MIB = 1 << 20


def with_partner(x, axis):
    return lax.ppermute(x, axis, [(i, i ^ 1) for i in range(lax.axis_size(axis))])


def with_other(x, axis):
    size = lax.axis_size(axis)
    return lax.ppermute(x, axis, [(i, (i + 1 if i % 2 else i - 1) % size) for i in range(size)])


def vmem():
    return pl.BlockSpec(memory_space=pltpu.VMEM)


def smem():
    return pl.BlockSpec(memory_space=pltpu.SMEM)


def call(kernel, mib, out_shape, in_specs, out_specs, scratch=()):
    return pl.pallas_call(
        kernel,
        out_shape=out_shape,
        in_specs=in_specs,
        out_specs=out_specs,
        scratch_shapes=list(scratch),
        compiler_params=pltpu.CompilerParams(vmem_limit_bytes=mib * MIB),
    )


def cut_kernel(x_ref, degree_ref, cols_ref, out_ref, dinv_ref, names_ref):
    rows = x_ref.shape[0]
    groups = rows // SUB
    square = (rows, rows)
    diagonal = lax.broadcasted_iota(jnp.int32, square, 0) == lax.broadcasted_iota(jnp.int32, square, 1)
    degree = jnp.sum(jnp.where(diagonal, degree_ref[...].astype(jnp.float32), 0.0), axis=1, keepdims=True)
    dinv = lax.rsqrt(degree)
    dinv_ref[...] = dinv
    names_ref[...] = jnp.zeros_like(names_ref)
    names_ref[:, pl.ds(0, cols_ref.shape[1])] = cols_ref[...].astype(jnp.float32)
    lane = lax.broadcasted_iota(jnp.int32, (rows, LANE), 1)
    note = jnp.where(lane < LANE // 2, names_ref[...], degree).reshape(groups, SUB, LANE).astype(jnp.bfloat16)
    for half in range(2):
        scaled = x_ref[:, half * LANE : (half + 1) * LANE].astype(jnp.float32) * dinv
        scaled = scaled.reshape(groups, SUB, LANE).astype(jnp.bfloat16)
        for a in range(groups):
            out_ref[half * groups + a, 0] = scaled[a]
            out_ref[half * groups + a, 1] = note[a]


def cut(features, degree, cols):
    rows = features.shape[0]
    return call(
        cut_kernel,
        60,
        (
            jax.ShapeDtypeStruct((2 * rows // SUB, 2, SUB, LANE), jnp.bfloat16),
            jax.ShapeDtypeStruct((rows, 1), jnp.float32),
        ),
        [vmem()] * 3,
        (vmem(), vmem()),
        [pltpu.VMEM((1, LANE), jnp.float32)],
    )(features, degree, cols)


def count_kernel(chunk, xk_ref, yk_ref, out_ref, acc_ref):
    edges = xk_ref.shape[1]
    tall = acc_ref.shape[0]
    wide = acc_ref.shape[1]
    for step in range(edges // chunk):
        xk = xk_ref[:, pl.ds(step * chunk, chunk)]
        yk = yk_ref[:, pl.ds(step * chunk, chunk)]
        left = (lax.broadcasted_iota(jnp.int32, (tall, chunk), 0) == xk).astype(jnp.float32).astype(jnp.bfloat16)
        right = (lax.broadcasted_iota(jnp.int32, (wide, chunk), 0) == yk).astype(jnp.float32).astype(jnp.bfloat16)
        part = lax.dot_general(left, right, (((1,), (1,)), ((), ())), preferred_element_type=jnp.float32)
        if step == 0:
            acc_ref[...] = part
        else:
            acc_ref[...] += part
    rows = out_ref.shape[0]
    for block in range(tall // rows):
        out_ref[:, pl.ds(block * wide, wide)] = acc_ref[pl.ds(block * rows, rows), :].astype(jnp.bfloat16)


def build_slab(row, key, rows, keys):
    wide = 256
    edges = row.shape[0]
    chunk = 768 if edges % 768 == 0 else 128
    tall = rows * (keys // wide)
    xk = ((key // wide) * rows + row).reshape(1, edges)
    yk = (key % wide).reshape(1, edges)
    return pl.pallas_call(
        functools.partial(count_kernel, chunk),
        out_shape=jax.ShapeDtypeStruct((rows, keys), jnp.bfloat16),
        in_specs=[vmem(), vmem()],
        out_specs=vmem(),
        scratch_shapes=[pltpu.VMEM((tall, wide), jnp.float32)],
        compiler_params=pltpu.CompilerParams(vmem_limit_bytes=24 * MIB),
        name="count",
    )(xk, yk)


def select_kernel(members, per_part, idx_ref, first_ref, own_ref, second_ref, out_ref, near_ref):
    listed = 3 * per_part
    near_ref[pl.ds(0, members)] = first_ref[...]
    near_ref[pl.ds(members, members)] = second_ref[...]

    def one(d, carry):
        for t in range(listed):
            at = idx_ref[d * listed + t]
            if t // per_part == 1:
                out_ref[d, t] = own_ref[jnp.bitwise_and(at, members - 1)]
            else:
                out_ref[d, t] = near_ref[jnp.bitwise_and(at, 2 * members - 1)]
        return carry

    lax.fori_loop(0, members, one, 0)


def select(idx, first, own, second, per_part):
    members = own.shape[0]
    return call(
        functools.partial(select_kernel, members, per_part),
        6,
        jax.ShapeDtypeStruct((members, 3 * per_part, SUB, LANE), own.dtype),
        [smem()] + [vmem()] * 3,
        vmem(),
        [pltpu.VMEM((2 * members, SUB, LANE), own.dtype)],
    )(idx, first, own, second)


def layer_kernel(listed, slab_ref, x_ref, weight_ref, dinv_ref, bias_ref, cot_ref, hid_ref, part_ref):
    dinv = dinv_ref[...]
    groups = part_ref.shape[1]
    span = listed * SUB
    rows = [jnp.dot(slab_ref[...], x_ref[half], preferred_element_type=jnp.float32) for half in range(2)]
    gathered = jnp.concatenate(rows, axis=1)
    high = gathered.astype(jnp.bfloat16)
    low = (gathered - high.astype(jnp.float32)).astype(jnp.bfloat16)
    weight = weight_ref[...]
    total = jnp.dot(high, weight, preferred_element_type=jnp.float32)
    total = total + jnp.dot(low, weight, preferred_element_type=jnp.float32)
    pre = total * dinv + bias_ref[...]
    sig = jax.nn.sigmoid(pre)
    hid_ref[...] = (pre * sig).astype(hid_ref.dtype)
    grad_pre = cot_ref[...].astype(jnp.float32) * sig * (1.0 + pre * (1.0 - sig))
    back = (grad_pre * dinv).astype(jnp.bfloat16)
    contract = (((0,), (0,)), ((), ()))
    grad = lax.dot_general(high, back, contract, preferred_element_type=jnp.float32)
    grad = grad + lax.dot_general(low, back, contract, preferred_element_type=jnp.float32)
    sums = jnp.sum(grad_pre, axis=0, keepdims=True)
    sums_high = sums.astype(jnp.bfloat16).astype(jnp.float32)
    sums_low = sums - sums_high
    at = lax.broadcasted_iota(jnp.int32, (SUB, LANE), 0)
    extra = jnp.zeros((SUB, LANE), jnp.float32)
    for index, value in enumerate((sums_high, sums_low)):
        for half in range(2):
            lanes = slice(half * LANE, (half + 1) * LANE)
            extra = jnp.where(at == 2 * index + half, value[:, lanes], extra)
    extra = extra.astype(jnp.bfloat16)
    for half in range(2):
        lanes = slice(half * LANE, (half + 1) * LANE)
        partial = lax.dot_general(slab_ref[...], back[:, lanes], contract, preferred_element_type=jnp.float32)
        for a in range(groups):
            piece = partial[a * span : (a + 1) * span, :].reshape(listed, SUB, LANE)
            part_ref[half, a, pl.ds(0, listed)] = piece.astype(jnp.bfloat16)
            part_ref[half, a, listed] = extra
            top = (half * groups + a) * SUB
            for other in range(2):
                block = grad[top : top + SUB, other * LANE : (other + 1) * LANE]
                part_ref[half, a, listed + 1 + other] = block.astype(jnp.bfloat16)


def layer(slab, x, weight, dinv, bias, cotangent, listed):
    rows, width = cotangent.shape
    shape = (2, rows // SUB, listed + 3, SUB, LANE)
    return call(
        functools.partial(layer_kernel, listed),
        16,
        (jax.ShapeDtypeStruct((rows, width), jnp.bfloat16), jax.ShapeDtypeStruct(shape, jnp.bfloat16)),
        [vmem()] * 6,
        (vmem(), vmem()),
    )(slab, x, weight, dinv, bias, cotangent)


def collect_kernel(members, per_part, parts, chains, idx_ref, got_ref, *refs):
    outs, acc_ref = refs[:-1], refs[-1]
    acc_ref[...] = jnp.zeros_like(acc_ref)
    tiles = acc_ref.shape[1]

    def some(step, carry):
        for part in parts:
            for t in range(part * per_part, (part + 1) * per_part):
                for j in range(chains):
                    d = step * chains + j
                    at = jnp.bitwise_and(idx_ref[d * 3 * per_part + t], tiles - 1)
                    acc_ref[j, at] += got_ref[d, t].astype(jnp.float32)
        return carry

    lax.fori_loop(0, members // chains, some, 0)
    for number, ref in enumerate(outs):
        part = pl.ds(number * members, members)
        value = acc_ref[0, part]
        for j in range(1, chains):
            value = value + acc_ref[j, part]
        ref[...] = value.astype(ref.dtype)


def collect(idx, parts, got, per_part, dtype):
    members = got.shape[0]
    chains = 4
    piece = (members, SUB, LANE)
    return call(
        functools.partial(collect_kernel, members, per_part, parts, chains),
        6,
        tuple(jax.ShapeDtypeStruct(piece, dtype) for _ in parts),
        [smem(), vmem()],
        (vmem(),) * len(parts),
        [pltpu.VMEM((chains, len(parts) * members, SUB, LANE), jnp.float32)],
    )(idx, got)


def join_kernel(got_ref, own_ref, first_ref, second_ref, share_ref, out_ref, bias_ref):
    members = own_ref.shape[0]
    total = share_ref[0]
    for ring in range(1, share_ref.shape[0]):
        total = total + share_ref[ring]
    for half in range(2):
        bias_ref[:, half * LANE : (half + 1) * LANE] = total[0, half : half + 1] + total[0, half + 2 : half + 3]
    rows = [total[1].astype(jnp.bfloat16), total[2].astype(jnp.bfloat16)]
    for m in range(members):
        dinv = lax.rsqrt(got_ref[m, 1].astype(jnp.float32)[:, LANE // 2 : LANE // 2 + 1])
        grad = own_ref[m] + first_ref[m].astype(jnp.float32) + second_ref[m].astype(jnp.float32)
        out_ref[m, 0] = (grad * dinv).astype(jnp.bfloat16)
        out_ref[m, 1] = rows[0]
        out_ref[m, 2] = rows[1]


def join(got, own, first, second, share):
    members = own.shape[0]
    return call(
        join_kernel,
        4,
        (
            jax.ShapeDtypeStruct((members, 3, SUB, LANE), jnp.bfloat16),
            jax.ShapeDtypeStruct((1, 2 * LANE), jnp.float32),
        ),
        [vmem()] * 5,
        (vmem(), vmem()),
    )(got, own, first, second, share)


def finish_kernel(final_ref, weight_ref, features_ref, weight_grad_ref):
    members = final_ref.shape[0]
    groups = members // 2
    sides = [final_ref[pl.ds(half * groups, groups), 0].astype(jnp.float32).reshape(-1, LANE) for half in range(2)]
    grad = jnp.concatenate(sides, axis=1).astype(jnp.bfloat16)
    features_ref[...] = lax.dot_general(
        grad, weight_ref[...], (((1,), (1,)), ((), ())), preferred_element_type=jnp.float32
    ).astype(features_ref.dtype)
    for half in range(2):
        rows = final_ref[:, 1 + half].astype(jnp.float32).reshape(-1, LANE)
        weight_grad_ref[:, half * LANE : (half + 1) * LANE] = rows


def finish(final, weight):
    width = weight.shape[0]
    rows = final.shape[0] // 2 * SUB
    return call(
        finish_kernel,
        6,
        (
            jax.ShapeDtypeStruct((rows, width), jnp.bfloat16),
            jax.ShapeDtypeStruct((width, width), jnp.float32),
        ),
        [vmem(), vmem()],
        (vmem(), vmem()),
    )(final, weight)


def swap(x, axis):
    return lax.all_to_all(x, axis, 0, 0, tiled=True)


def per_device(features, weight, bias, cotangent, degree, tile_cols, edge_tile, edge_row, edge_col):
    rows, _ = features.shape
    members = lax.axis_size("grp")
    rings = lax.axis_size("rep")
    listed = tile_cols.shape[1]
    per_part = listed // 3

    payload, dinv = cut(features, degree[None, :], tile_cols)
    got = swap(payload, "grp")
    own = got[:, 0]
    first = with_partner(own, "rep")
    second = with_other(own, "rep")

    names = got[:, 1, 0, :listed].astype(jnp.int32)
    part = lax.broadcasted_iota(jnp.int32, names.shape, 1) // per_part
    even = lax.axis_index("rep") % 2 == 0
    late = jnp.where(even, part == 0, part == 2)
    idx = (names % members + jnp.where(late, members, 0)).reshape(-1)

    tile = edge_tile[0]
    col = edge_col[0]
    key = (col // SUB) * (listed * SUB) + tile * SUB + col % SUB
    slab = build_slab(edge_row[0], key, rows, listed * rows)

    window = swap(select(idx, first, own, second, per_part), "grp")
    hidden, partial = layer(
        slab, window.reshape(2, listed * rows, LANE), weight, dinv, bias[None, :], cotangent, listed
    )
    mine = swap(partial.reshape(members, listed + 3, SUB, LANE), "grp")

    share = mine[:, listed:].astype(jnp.float32).sum(axis=0)
    share = swap(jnp.broadcast_to(share[None], (rings, 3, SUB, LANE)), "rep")
    to_first, to_second = collect(idx, (0, 2), mine, per_part, jnp.bfloat16)
    from_first = with_partner(to_first, "rep")
    from_second = with_other(to_second, "rep")
    (own_sum,) = collect(idx, (1,), mine, per_part, jnp.float32)

    final, grad_bias = join(got, own_sum, from_first, from_second, share)
    final = swap(final, "grp")
    grad_features, grad_weight = finish(final, weight)
    return (hidden, grad_features, grad_weight, grad_bias[0])


def solution(mesh):
    return jax.shard_map(
        per_device,
        mesh=mesh,
        in_specs=(
            P(("rep", "grp"), None),
            P(),
            P(),
            P(("rep", "grp"), None),
            P(("rep", "grp")),
            P(("rep", "grp"), None),
            P(("rep", "grp"), None),
            P(("rep", "grp"), None),
            P(("rep", "grp"), None),
        ),
        out_specs=(P(("rep", "grp"), None), P(("rep", "grp"), None), P(), P()),
        check_vma=False,
    )
```

```python
import functools

import jax
import jax.numpy as jnp
from jax import lax
from jax.experimental import pallas as pl
from jax.experimental.pallas import tpu as pltpu
from jax.sharding import PartitionSpec as P


SUB = 8
LANE = 128
SEGMENT = 8
MIB = 1 << 20


def with_partner(x, axis):
    return lax.ppermute(x, axis, [(i, i ^ 1) for i in range(lax.axis_size(axis))])


def with_other(x, axis):
    size = lax.axis_size(axis)
    return lax.ppermute(x, axis, [(i, (i + 1 if i % 2 else i - 1) % size) for i in range(size)])


def vmem():
    return pl.BlockSpec(memory_space=pltpu.VMEM)


def smem():
    return pl.BlockSpec(memory_space=pltpu.SMEM)


def hbm():
    return pl.BlockSpec(memory_space=pltpu.HBM)


def call(kernel, mib, out_shape, in_specs, out_specs, scratch=()):
    return pl.pallas_call(
        kernel,
        out_shape=out_shape,
        in_specs=in_specs,
        out_specs=out_specs,
        scratch_shapes=list(scratch),
        compiler_params=pltpu.CompilerParams(vmem_limit_bytes=mib * MIB),
    )


def cut_kernel(x_ref, degree_ref, cols_ref, out_ref, dinv_ref, names_ref):
    rows = x_ref.shape[0]
    groups = rows // SUB
    square = (rows, rows)
    diagonal = lax.broadcasted_iota(jnp.int32, square, 0) == lax.broadcasted_iota(jnp.int32, square, 1)
    degree = jnp.sum(jnp.where(diagonal, degree_ref[...].astype(jnp.float32), 0.0), axis=1, keepdims=True)
    dinv = lax.rsqrt(degree)
    dinv_ref[...] = dinv
    names_ref[...] = jnp.zeros_like(names_ref)
    names_ref[:, pl.ds(0, cols_ref.shape[1])] = cols_ref[...].astype(jnp.float32)
    lane = lax.broadcasted_iota(jnp.int32, (rows, LANE), 1)
    note = jnp.where(lane < LANE // 2, names_ref[...], degree).reshape(groups, SUB, LANE).astype(jnp.bfloat16)
    members = out_ref.shape[0]
    for half in range(2):
        scaled = x_ref[:, half * LANE : (half + 1) * LANE].astype(jnp.float32) * dinv
        scaled = scaled.reshape(groups, SUB, LANE).astype(jnp.bfloat16)
        for q in range(members):
            for sub in range(2):
                out_ref[q, 2 * half + sub] = scaled[2 * (q % SEGMENT) + sub]
        for a in range(groups):
            out_ref[half * groups + a, 4] = note[a]


def cut(features, degree, cols):
    rows = features.shape[0]
    return call(
        cut_kernel,
        60,
        (
            jax.ShapeDtypeStruct((2 * rows // SUB, 5, SUB, LANE), jnp.bfloat16),
            jax.ShapeDtypeStruct((rows, 1), jnp.float32),
        ),
        [vmem()] * 3,
        (vmem(), vmem()),
        [pltpu.VMEM((1, LANE), jnp.float32)],
    )(features, degree, cols)


def count_kernel(chunk, xk_ref, yk_ref, out_ref, acc_ref):
    edges = xk_ref.shape[1]
    tall = acc_ref.shape[0]
    wide = acc_ref.shape[1]
    for step in range(edges // chunk):
        xk = xk_ref[:, pl.ds(step * chunk, chunk)]
        yk = yk_ref[:, pl.ds(step * chunk, chunk)]
        left = (lax.broadcasted_iota(jnp.int32, (tall, chunk), 0) == xk).astype(jnp.float32).astype(jnp.bfloat16)
        right = (lax.broadcasted_iota(jnp.int32, (wide, chunk), 0) == yk).astype(jnp.float32).astype(jnp.bfloat16)
        part = lax.dot_general(left, right, (((1,), (1,)), ((), ())), preferred_element_type=jnp.float32)
        if step == 0:
            acc_ref[...] = part
        else:
            acc_ref[...] += part
    rows = out_ref.shape[0]
    for block in range(tall // rows):
        out_ref[:, pl.ds(block * wide, wide)] = acc_ref[pl.ds(block * rows, rows), :].astype(jnp.bfloat16)


def build_slab(row, key, rows, keys):
    wide = 256
    edges = row.shape[0]
    chunk = 768 if edges % 768 == 0 else 128
    tall = rows * (keys // wide)
    xk = ((key // wide) * rows + row).reshape(1, edges)
    yk = (key % wide).reshape(1, edges)
    return pl.pallas_call(
        functools.partial(count_kernel, chunk),
        out_shape=jax.ShapeDtypeStruct((rows, keys), jnp.bfloat16),
        in_specs=[vmem(), vmem()],
        out_specs=vmem(),
        scratch_shapes=[pltpu.VMEM((tall, wide), jnp.float32)],
        compiler_params=pltpu.CompilerParams(vmem_limit_bytes=24 * MIB),
        name="count",
    )(xk, yk)


def select_own_kernel(per_part, idx_ref, own_ref, out_ref, made_ref, sem):
    members = own_ref.shape[0]
    for d in range(SEGMENT):
        for t in range(per_part):
            at = jnp.bitwise_and(idx_ref[d * 3 * per_part + per_part + t], members - 1)
            made_ref[d, t] = own_ref[at]
    copy = pltpu.make_async_copy(made_ref, out_ref, sem)
    copy.start()
    copy.wait()


def select_own(idx, own, per_part):
    shape = (SEGMENT, per_part) + own.shape[1:]
    return call(
        functools.partial(select_own_kernel, per_part),
        6,
        jax.ShapeDtypeStruct(shape, own.dtype),
        [smem(), vmem()],
        hbm(),
        [pltpu.VMEM(shape, own.dtype), pltpu.SemaphoreType.DMA],
    )(idx, own)


def select_far_kernel(per_part, idx_ref, first_ref, second_ref, out_ref, near_ref):
    members = first_ref.shape[0]
    near_ref[pl.ds(0, members)] = first_ref[...]
    near_ref[pl.ds(members, members)] = second_ref[...]
    for d in range(SEGMENT):
        for t in range(2 * per_part):
            place = t if t < per_part else t + per_part
            at = jnp.bitwise_and(idx_ref[d * 3 * per_part + place], 2 * members - 1)
            out_ref[d, t] = near_ref[at]


def select_far(idx, first, second, per_part):
    members = first.shape[0]
    return call(
        functools.partial(select_far_kernel, per_part),
        6,
        jax.ShapeDtypeStruct((SEGMENT, 2 * per_part) + first.shape[1:], first.dtype),
        [smem(), vmem(), vmem()],
        vmem(),
        [pltpu.VMEM((2 * members,) + first.shape[1:], first.dtype)],
    )(idx, first, second)


def layer_kernel(listed, slab_ref, xown_ref, xfar_ref, weight_ref, dinv_ref, bias_ref, cot_ref, hid_ref, part_ref):
    dinv = dinv_ref[...]
    groups = part_ref.shape[1]
    per_part = listed // 3
    tall = 2 * SUB
    edge = xown_ref.shape[0] * tall
    rows = []
    for half in range(2):
        near = xown_ref[:, half].reshape(edge, LANE)
        far = xfar_ref[:, half].reshape(2 * edge, LANE)
        total = jnp.dot(slab_ref[:, :edge], near, preferred_element_type=jnp.float32)
        rows.append(total + jnp.dot(slab_ref[:, edge:], far, preferred_element_type=jnp.float32))
    gathered = jnp.concatenate(rows, axis=1)
    high = gathered.astype(jnp.bfloat16)
    low = (gathered - high.astype(jnp.float32)).astype(jnp.bfloat16)
    weight = weight_ref[...]
    total = jnp.dot(high, weight, preferred_element_type=jnp.float32)
    total = total + jnp.dot(low, weight, preferred_element_type=jnp.float32)
    pre = total * dinv + bias_ref[...]
    sig = jax.nn.sigmoid(pre)
    hid_ref[...] = (pre * sig).astype(hid_ref.dtype)
    grad_pre = cot_ref[...].astype(jnp.float32) * sig * (1.0 + pre * (1.0 - sig))
    back = (grad_pre * dinv).astype(jnp.bfloat16)
    contract = (((0,), (0,)), ((), ()))
    grad = lax.dot_general(high, back, contract, preferred_element_type=jnp.float32)
    grad = grad + lax.dot_general(low, back, contract, preferred_element_type=jnp.float32)
    sums = jnp.sum(grad_pre, axis=0, keepdims=True)
    sums_high = sums.astype(jnp.bfloat16).astype(jnp.float32)
    sums_low = sums - sums_high
    at = lax.broadcasted_iota(jnp.int32, (SUB, LANE), 0)
    extra = jnp.zeros((SUB, LANE), jnp.float32)
    for index, value in enumerate((sums_high, sums_low)):
        for half in range(2):
            lanes = slice(half * LANE, (half + 1) * LANE)
            extra = jnp.where(at == 2 * index + half, value[:, lanes], extra)
    extra = extra.astype(jnp.bfloat16)
    for half in range(2):
        lanes = slice(half * LANE, (half + 1) * LANE)
        partial = lax.dot_general(slab_ref[...], back[:, lanes], contract, preferred_element_type=jnp.float32)
        for holder in range(groups // 2):
            at = holder * per_part * tall
            near = partial[at : at + per_part * tall].reshape(per_part, 2, SUB, LANE)
            at = edge + 2 * at
            far = partial[at : at + 2 * per_part * tall].reshape(2 * per_part, 2, SUB, LANE)
            for sub in range(2):
                a = 2 * holder + sub
                part_ref[half, a, pl.ds(0, per_part)] = far[:per_part, sub].astype(jnp.bfloat16)
                part_ref[half, a, pl.ds(per_part, per_part)] = near[:, sub].astype(jnp.bfloat16)
                part_ref[half, a, pl.ds(2 * per_part, per_part)] = far[per_part:, sub].astype(jnp.bfloat16)
        for a in range(groups):
            part_ref[half, a, listed] = extra
            top = (half * groups + a) * SUB
            for other in range(2):
                block = grad[top : top + SUB, other * LANE : (other + 1) * LANE]
                part_ref[half, a, listed + 1 + other] = block.astype(jnp.bfloat16)


def layer(slab, xown, xfar, weight, dinv, bias, cotangent, listed):
    rows, width = cotangent.shape
    shape = (2, rows // SUB, listed + 3, SUB, LANE)
    return call(
        functools.partial(layer_kernel, listed),
        16,
        (jax.ShapeDtypeStruct((rows, width), jnp.bfloat16), jax.ShapeDtypeStruct(shape, jnp.bfloat16)),
        [vmem()] * 7,
        (vmem(), vmem()),
    )(slab, xown, xfar, weight, dinv, bias, cotangent)


def collect_kernel(members, per_part, parts, chains, idx_ref, got_ref, *refs):
    outs, acc_ref = refs[:-1], refs[-1]
    acc_ref[...] = jnp.zeros_like(acc_ref)
    tiles = acc_ref.shape[1]

    def some(step, carry):
        for part in parts:
            for t in range(part * per_part, (part + 1) * per_part):
                for j in range(chains):
                    d = step * chains + j
                    at = jnp.bitwise_and(idx_ref[d * 3 * per_part + t], tiles - 1)
                    acc_ref[j, at] += got_ref[d, t].astype(jnp.float32)
        return carry

    lax.fori_loop(0, members // chains, some, 0)
    for number, ref in enumerate(outs):
        part = pl.ds(number * members, members)
        value = acc_ref[0, part]
        for j in range(1, chains):
            value = value + acc_ref[j, part]
        ref[...] = value.astype(ref.dtype)


def collect(idx, parts, got, per_part, dtype):
    members = got.shape[0]
    chains = 4
    piece = (members, SUB, LANE)
    return call(
        functools.partial(collect_kernel, members, per_part, parts, chains),
        6,
        tuple(jax.ShapeDtypeStruct(piece, dtype) for _ in parts),
        [smem(), vmem()],
        (vmem(),) * len(parts),
        [pltpu.VMEM((chains, len(parts) * members, SUB, LANE), jnp.float32)],
    )(idx, got)


def join_kernel(got_ref, own_ref, first_ref, second_ref, share_ref, out_ref, bias_ref):
    members = own_ref.shape[0]
    total = share_ref[0]
    for ring in range(1, share_ref.shape[0]):
        total = total + share_ref[ring]
    for half in range(2):
        bias_ref[:, half * LANE : (half + 1) * LANE] = total[0, half : half + 1] + total[0, half + 2 : half + 3]
    rows = [total[1].astype(jnp.bfloat16), total[2].astype(jnp.bfloat16)]
    for m in range(members):
        dinv = lax.rsqrt(got_ref[m, 4].astype(jnp.float32)[:, LANE // 2 : LANE // 2 + 1])
        grad = own_ref[m] + first_ref[m].astype(jnp.float32) + second_ref[m].astype(jnp.float32)
        out_ref[m, 0] = (grad * dinv).astype(jnp.bfloat16)
        out_ref[m, 1] = rows[0]
        out_ref[m, 2] = rows[1]


def join(got, own, first, second, share):
    members = own.shape[0]
    return call(
        join_kernel,
        4,
        (
            jax.ShapeDtypeStruct((members, 3, SUB, LANE), jnp.bfloat16),
            jax.ShapeDtypeStruct((1, 2 * LANE), jnp.float32),
        ),
        [vmem()] * 5,
        (vmem(), vmem()),
    )(got, own, first, second, share)


def finish_kernel(final_ref, weight_ref, features_ref, weight_grad_ref):
    members = final_ref.shape[0]
    groups = members // 2
    sides = [final_ref[pl.ds(half * groups, groups), 0].astype(jnp.float32).reshape(-1, LANE) for half in range(2)]
    grad = jnp.concatenate(sides, axis=1).astype(jnp.bfloat16)
    features_ref[...] = lax.dot_general(
        grad, weight_ref[...], (((1,), (1,)), ((), ())), preferred_element_type=jnp.float32
    ).astype(features_ref.dtype)
    for half in range(2):
        rows = final_ref[:, 1 + half].astype(jnp.float32).reshape(-1, LANE)
        weight_grad_ref[:, half * LANE : (half + 1) * LANE] = rows


def finish(final, weight):
    width = weight.shape[0]
    rows = final.shape[0] // 2 * SUB
    return call(
        finish_kernel,
        6,
        (
            jax.ShapeDtypeStruct((rows, width), jnp.bfloat16),
            jax.ShapeDtypeStruct((width, width), jnp.float32),
        ),
        [vmem(), vmem()],
        (vmem(), vmem()),
    )(final, weight)


def swap(x, axis):
    return lax.all_to_all(x, axis, 0, 0, tiled=True)


def segment_swap(x, members):
    groups = [list(range(first, first + SEGMENT)) for first in range(0, members, SEGMENT)]
    return lax.all_to_all(x, "grp", 0, 0, axis_index_groups=groups, tiled=True)


def per_device(features, weight, bias, cotangent, degree, tile_cols, edge_tile, edge_row, edge_col):
    rows, _ = features.shape
    members = lax.axis_size("grp")
    rings = lax.axis_size("rep")
    listed = tile_cols.shape[1]
    per_part = listed // 3

    payload, dinv = cut(features, degree[None, :], tile_cols)
    got = swap(payload, "grp")
    own = got[:, :4]
    first = with_partner(own, "rep")
    second = with_other(own, "rep")

    names = got[:, 4, 0, :listed].astype(jnp.int32)
    part = lax.broadcasted_iota(jnp.int32, names.shape, 1) // per_part
    even = lax.axis_index("rep") % 2 == 0
    late = jnp.where(even, part == 0, part == 2)
    idx = names % members + jnp.where(late, members, 0)
    segment = lax.axis_index("grp") // SEGMENT
    idx = idx.reshape(-1)
    near_idx = lax.dynamic_slice_in_dim(idx, segment * SEGMENT * listed, SEGMENT * listed, 0)

    tile = edge_tile[0]
    col = edge_col[0]
    tall = 2 * SUB
    far_tile = jnp.where(tile < per_part, tile, tile - per_part)
    is_own = (tile >= per_part) & (tile < 2 * per_part)
    own_key = (col // tall * per_part + tile - per_part) * tall
    far_key = per_part * rows + (col // tall * 2 * per_part + far_tile) * tall
    key = jnp.where(is_own, own_key, far_key) + col % tall
    slab = build_slab(edge_row[0], key, rows, listed * rows)

    chosen_own = select_own(near_idx, own, per_part)
    window_own = segment_swap(chosen_own, members)
    window_far = segment_swap(select_far(near_idx, first, second, per_part), members)
    hidden, partial = layer(
        slab,
        window_own.reshape(rows // tall * per_part, 2, tall, LANE),
        window_far.reshape(rows // tall * 2 * per_part, 2, tall, LANE),
        weight,
        dinv,
        bias[None, :],
        cotangent,
        listed,
    )
    mine = swap(partial.reshape(members, listed + 3, SUB, LANE), "grp")

    share = mine[:, listed:].astype(jnp.float32).sum(axis=0)
    share = swap(jnp.broadcast_to(share[None], (rings, 3, SUB, LANE)), "rep")
    to_first, to_second = collect(idx, (0, 2), mine, per_part, jnp.bfloat16)
    from_first = with_partner(to_first, "rep")
    from_second = with_other(to_second, "rep")
    (own_sum,) = collect(idx, (1,), mine, per_part, jnp.float32)

    final, grad_bias = join(got, own_sum, from_first, from_second, share)
    final = swap(final, "grp")
    grad_features, grad_weight = finish(final, weight)
    return (hidden, grad_features, grad_weight, grad_bias[0])


def solution(mesh):
    return jax.shard_map(
        per_device,
        mesh=mesh,
        in_specs=(
            P(("rep", "grp"), None),
            P(),
            P(),
            P(("rep", "grp"), None),
            P(("rep", "grp")),
            P(("rep", "grp"), None),
            P(("rep", "grp"), None),
            P(("rep", "grp"), None),
            P(("rep", "grp"), None),
        ),
        out_specs=(P(("rep", "grp"), None), P(("rep", "grp"), None), P(), P()),
        check_vma=False,
    )
```

```python
import functools

import jax
import jax.numpy as jnp
from jax import lax
from jax.experimental import pallas as pl
from jax.experimental.pallas import tpu as pltpu
from jax.sharding import PartitionSpec as P


SUB = 8
LANE = 128
SEGMENT = 8
MIB = 1 << 20


def with_partner(x, axis):
    return lax.ppermute(x, axis, [(i, i ^ 1) for i in range(lax.axis_size(axis))])


def with_other(x, axis):
    size = lax.axis_size(axis)
    return lax.ppermute(x, axis, [(i, (i + 1 if i % 2 else i - 1) % size) for i in range(size)])


def vmem():
    return pl.BlockSpec(memory_space=pltpu.VMEM)


def smem():
    return pl.BlockSpec(memory_space=pltpu.SMEM)


def hbm():
    return pl.BlockSpec(memory_space=pltpu.HBM)


def call(kernel, mib, out_shape, in_specs, out_specs, scratch=()):
    return pl.pallas_call(
        kernel,
        out_shape=out_shape,
        in_specs=in_specs,
        out_specs=out_specs,
        scratch_shapes=list(scratch),
        compiler_params=pltpu.CompilerParams(vmem_limit_bytes=mib * MIB),
    )


def cut_kernel(x_ref, degree_ref, cols_ref, out_ref, dinv_ref, names_ref):
    rows = x_ref.shape[0]
    groups = rows // SUB
    square = (rows, rows)
    diagonal = lax.broadcasted_iota(jnp.int32, square, 0) == lax.broadcasted_iota(jnp.int32, square, 1)
    degree = jnp.sum(jnp.where(diagonal, degree_ref[...].astype(jnp.float32), 0.0), axis=1, keepdims=True)
    dinv = lax.rsqrt(degree)
    dinv_ref[...] = dinv
    names_ref[...] = jnp.zeros_like(names_ref)
    names_ref[:, pl.ds(0, cols_ref.shape[1])] = cols_ref[...].astype(jnp.float32)
    lane = lax.broadcasted_iota(jnp.int32, (rows, LANE), 1)
    note = jnp.where(lane < LANE // 2, names_ref[...], degree).reshape(groups, SUB, LANE).astype(jnp.bfloat16)
    members = out_ref.shape[0]
    for half in range(2):
        scaled = x_ref[:, half * LANE : (half + 1) * LANE].astype(jnp.float32) * dinv
        scaled = scaled.reshape(groups, SUB, LANE).astype(jnp.bfloat16)
        for q in range(members):
            for sub in range(2):
                out_ref[q, 2 * half + sub] = scaled[2 * (q % SEGMENT) + sub]
        for a in range(groups):
            out_ref[half * groups + a, 4] = note[a]


def cut(features, degree, cols):
    rows = features.shape[0]
    return call(
        cut_kernel,
        60,
        (
            jax.ShapeDtypeStruct((2 * rows // SUB, 5, SUB, LANE), jnp.bfloat16),
            jax.ShapeDtypeStruct((rows, 1), jnp.float32),
        ),
        [vmem()] * 3,
        (vmem(), vmem()),
        [pltpu.VMEM((1, LANE), jnp.float32)],
    )(features, degree, cols)


def count_kernel(chunk, xk_ref, yk_ref, out_ref, acc_ref):
    edges = xk_ref.shape[1]
    tall = acc_ref.shape[0]
    wide = acc_ref.shape[1]
    for step in range(edges // chunk):
        xk = xk_ref[:, pl.ds(step * chunk, chunk)]
        yk = yk_ref[:, pl.ds(step * chunk, chunk)]
        left = (lax.broadcasted_iota(jnp.int32, (tall, chunk), 0) == xk).astype(jnp.float32).astype(jnp.bfloat16)
        right = (lax.broadcasted_iota(jnp.int32, (wide, chunk), 0) == yk).astype(jnp.float32).astype(jnp.bfloat16)
        part = lax.dot_general(left, right, (((1,), (1,)), ((), ())), preferred_element_type=jnp.float32)
        if step == 0:
            acc_ref[...] = part
        else:
            acc_ref[...] += part
    rows = out_ref.shape[0]
    for block in range(tall // rows):
        out_ref[:, pl.ds(block * wide, wide)] = acc_ref[pl.ds(block * rows, rows), :].astype(jnp.bfloat16)


def build_slab(row, key, rows, keys):
    wide = 256
    edges = row.shape[0]
    chunk = 768 if edges % 768 == 0 else 128
    tall = rows * (keys // wide)
    xk = ((key // wide) * rows + row).reshape(1, edges)
    yk = (key % wide).reshape(1, edges)
    return pl.pallas_call(
        functools.partial(count_kernel, chunk),
        out_shape=jax.ShapeDtypeStruct((rows, keys), jnp.bfloat16),
        in_specs=[vmem(), vmem()],
        out_specs=vmem(),
        scratch_shapes=[pltpu.VMEM((tall, wide), jnp.float32)],
        compiler_params=pltpu.CompilerParams(vmem_limit_bytes=24 * MIB),
        name="count",
    )(xk, yk)


def select_own_kernel(per_part, idx_ref, own_ref, out_ref, made_ref, sem):
    members = own_ref.shape[0]
    for d in range(SEGMENT):
        for t in range(per_part):
            at = jnp.bitwise_and(idx_ref[d * 3 * per_part + per_part + t], members - 1)
            made_ref[d, t] = own_ref[at]
    copy = pltpu.make_async_copy(made_ref, out_ref, sem)
    copy.start()
    copy.wait()


def select_own(idx, own, per_part):
    shape = (SEGMENT, per_part) + own.shape[1:]
    return call(
        functools.partial(select_own_kernel, per_part),
        6,
        jax.ShapeDtypeStruct(shape, own.dtype),
        [smem(), vmem()],
        hbm(),
        [pltpu.VMEM(shape, own.dtype), pltpu.SemaphoreType.DMA],
    )(idx, own)


def select_far_kernel(per_part, idx_ref, first_ref, second_ref, out_ref, near_ref):
    members = first_ref.shape[0]
    near_ref[pl.ds(0, members)] = first_ref[...]
    near_ref[pl.ds(members, members)] = second_ref[...]
    for d in range(SEGMENT):
        for t in range(2 * per_part):
            place = t if t < per_part else t + per_part
            at = jnp.bitwise_and(idx_ref[d * 3 * per_part + place], 2 * members - 1)
            out_ref[d, t] = near_ref[at]


def select_far(idx, first, second, per_part):
    members = first.shape[0]
    return call(
        functools.partial(select_far_kernel, per_part),
        6,
        jax.ShapeDtypeStruct((SEGMENT, 2 * per_part) + first.shape[1:], first.dtype),
        [smem(), vmem(), vmem()],
        vmem(),
        [pltpu.VMEM((2 * members,) + first.shape[1:], first.dtype)],
    )(idx, first, second)


def layer_kernel(listed, slab_ref, xown_ref, xfar_ref, weight_ref, dinv_ref, bias_ref, cot_ref, hid_ref, part_ref, out_ref, grad_ref, sem):
    dinv = dinv_ref[...]
    members = grad_ref.shape[0]
    per_part = listed // 3
    tall = 2 * SUB
    edge = xown_ref.shape[0] * tall
    rows = []
    for half in range(2):
        near = xown_ref[:, half].reshape(edge, LANE)
        far = xfar_ref[:, half].reshape(2 * edge, LANE)
        total = jnp.dot(slab_ref[:, :edge], near, preferred_element_type=jnp.float32)
        rows.append(total + jnp.dot(slab_ref[:, edge:], far, preferred_element_type=jnp.float32))
    gathered = jnp.concatenate(rows, axis=1)
    high = gathered.astype(jnp.bfloat16)
    low = (gathered - high.astype(jnp.float32)).astype(jnp.bfloat16)
    weight = weight_ref[...]
    total = jnp.dot(high, weight, preferred_element_type=jnp.float32)
    total = total + jnp.dot(low, weight, preferred_element_type=jnp.float32)
    pre = total * dinv + bias_ref[...]
    sig = jax.nn.sigmoid(pre)
    hid_ref[...] = (pre * sig).astype(hid_ref.dtype)
    grad_pre = cot_ref[...].astype(jnp.float32) * sig * (1.0 + pre * (1.0 - sig))
    back = (grad_pre * dinv).astype(jnp.bfloat16)
    contract = (((0,), (0,)), ((), ()))
    grad = lax.dot_general(high, back, contract, preferred_element_type=jnp.float32)
    grad = grad + lax.dot_general(low, back, contract, preferred_element_type=jnp.float32)
    sums = jnp.sum(grad_pre, axis=0, keepdims=True)
    sums_high = sums.astype(jnp.bfloat16).astype(jnp.float32)
    sums_low = sums - sums_high
    at = lax.broadcasted_iota(jnp.int32, (SUB, LANE), 0)
    extra = jnp.zeros((SUB, LANE), jnp.float32)
    for index, value in enumerate((sums_high, sums_low)):
        for half in range(2):
            lanes = slice(half * LANE, (half + 1) * LANE)
            extra = jnp.where(at == 2 * index + half, value[:, lanes], extra)
    extra = extra.astype(jnp.bfloat16)
    for q in range(members):
        grad_ref[q, 0] = extra
        for half in range(2):
            block = grad[q * SUB : (q + 1) * SUB, half * LANE : (half + 1) * LANE]
            grad_ref[q, 1 + half] = block.astype(jnp.bfloat16)
    copy = pltpu.make_async_copy(grad_ref, out_ref, sem)
    copy.start()
    for half in range(2):
        lanes = slice(half * LANE, (half + 1) * LANE)
        pair = pl.ds(2 * half, 2)
        partial = lax.dot_general(slab_ref[...], back[:, lanes], contract, preferred_element_type=jnp.float32)
        for holder in range(SEGMENT):
            at = holder * per_part * tall
            near = partial[at : at + per_part * tall].reshape(per_part, 2, SUB, LANE).astype(jnp.bfloat16)
            at = edge + 2 * at
            far = partial[at : at + 2 * per_part * tall].reshape(2 * per_part, 2, SUB, LANE).astype(jnp.bfloat16)
            part_ref[holder, pl.ds(0, per_part), pair] = far[:per_part]
            part_ref[holder, pl.ds(per_part, per_part), pair] = near
            part_ref[holder, pl.ds(2 * per_part, per_part), pair] = far[per_part:]
    copy.wait()


def layer(slab, xown, xfar, weight, dinv, bias, cotangent, members, listed):
    rows, width = cotangent.shape
    grad = (members, 3, SUB, LANE)
    return call(
        functools.partial(layer_kernel, listed),
        16,
        (
            jax.ShapeDtypeStruct((rows, width), jnp.bfloat16),
            jax.ShapeDtypeStruct((SEGMENT, listed, 4, SUB, LANE), jnp.bfloat16),
            jax.ShapeDtypeStruct(grad, jnp.bfloat16),
        ),
        [vmem()] * 7,
        (vmem(), vmem(), hbm()),
        [pltpu.VMEM(grad, jnp.bfloat16), pltpu.SemaphoreType.DMA],
    )(slab, xown, xfar, weight, dinv, bias, cotangent)


def collect_kernel(members, per_part, parts, chains, idx_ref, got_ref, *refs):
    outs, acc_ref = refs[:-1], refs[-1]
    acc_ref[...] = jnp.zeros_like(acc_ref)
    tiles = acc_ref.shape[1]
    for step in range(SEGMENT // chains):
        for part in parts:
            for t in range(part * per_part, (part + 1) * per_part):
                for j in range(chains):
                    d = step * chains + j
                    at = jnp.bitwise_and(idx_ref[d * 3 * per_part + t], tiles - 1)
                    acc_ref[j, at] += got_ref[d, t].astype(jnp.float32)
    for number, ref in enumerate(outs):
        part = pl.ds(number * members, members)
        value = acc_ref[0, part]
        for j in range(1, chains):
            value = value + acc_ref[j, part]
        ref[...] = value.astype(ref.dtype)


def collect(idx, parts, got, members, per_part, dtype):
    chains = 2
    piece = (members,) + got.shape[2:]
    return call(
        functools.partial(collect_kernel, members, per_part, parts, chains),
        8,
        tuple(jax.ShapeDtypeStruct(piece, dtype) for _ in parts),
        [smem(), vmem()],
        (vmem(),) * len(parts),
        [pltpu.VMEM((chains, len(parts) * members) + got.shape[2:], jnp.float32)],
    )(idx, got)


def join_kernel(own_ref, first_ref, second_ref, share_ref, out_ref, bias_ref):
    members = own_ref.shape[0]
    total = share_ref[0]
    for ring in range(1, share_ref.shape[0]):
        total = total + share_ref[ring]
    for half in range(2):
        bias_ref[:, half * LANE : (half + 1) * LANE] = total[0, half : half + 1] + total[0, half + 2 : half + 3]
    rows = [total[1].astype(jnp.bfloat16), total[2].astype(jnp.bfloat16)]
    for m in range(members):
        grad = own_ref[m] + first_ref[m].astype(jnp.float32) + second_ref[m].astype(jnp.float32)
        out_ref[m, pl.ds(0, 4)] = grad.astype(jnp.bfloat16)
        out_ref[m, 4] = rows[0]
        out_ref[m, 5] = rows[1]


def join(own, first, second, share):
    members = own.shape[0]
    return call(
        join_kernel,
        6,
        (
            jax.ShapeDtypeStruct((members, 6, SUB, LANE), jnp.bfloat16),
            jax.ShapeDtypeStruct((1, 2 * LANE), jnp.float32),
        ),
        [vmem()] * 4,
        (vmem(), vmem()),
    )(own, first, second, share)


def finish_kernel(final_ref, dinv_ref, weight_ref, features_ref, weight_grad_ref):
    members = final_ref.shape[0]
    dinv = dinv_ref[...]
    sides = []
    for half in range(2):
        pair = pl.ds(2 * half, 2)
        total = final_ref[pl.ds(0, SEGMENT), pair].astype(jnp.float32)
        for first in range(SEGMENT, members, SEGMENT):
            total = total + final_ref[pl.ds(first, SEGMENT), pair].astype(jnp.float32)
        sides.append(total.reshape(-1, LANE) * dinv)
    grad = jnp.concatenate(sides, axis=1).astype(jnp.bfloat16)
    features_ref[...] = lax.dot_general(
        grad, weight_ref[...], (((1,), (1,)), ((), ())), preferred_element_type=jnp.float32
    ).astype(features_ref.dtype)
    for half in range(2):
        rows = final_ref[:, 4 + half].astype(jnp.float32).reshape(-1, LANE)
        weight_grad_ref[:, half * LANE : (half + 1) * LANE] = rows


def finish(final, dinv, weight):
    width = weight.shape[0]
    rows = dinv.shape[0]
    return call(
        finish_kernel,
        6,
        (
            jax.ShapeDtypeStruct((rows, width), jnp.bfloat16),
            jax.ShapeDtypeStruct((width, width), jnp.float32),
        ),
        [vmem()] * 3,
        (vmem(), vmem()),
    )(final, dinv, weight)


def swap(x, axis):
    return lax.all_to_all(x, axis, 0, 0, tiled=True)


def segment_swap(x, members):
    groups = [list(range(first, first + SEGMENT)) for first in range(0, members, SEGMENT)]
    return lax.all_to_all(x, "grp", 0, 0, axis_index_groups=groups, tiled=True)


def per_device(features, weight, bias, cotangent, degree, tile_cols, edge_tile, edge_row, edge_col):
    rows, _ = features.shape
    members = lax.axis_size("grp")
    rings = lax.axis_size("rep")
    listed = tile_cols.shape[1]
    per_part = listed // 3

    payload, dinv = cut(features, degree[None, :], tile_cols)
    got = swap(payload, "grp")
    own = got[:, :4]
    first = with_partner(own, "rep")
    second = with_other(own, "rep")

    names = got[:, 4, 0, :listed].astype(jnp.int32)
    part = lax.broadcasted_iota(jnp.int32, names.shape, 1) // per_part
    even = lax.axis_index("rep") % 2 == 0
    late = jnp.where(even, part == 0, part == 2)
    idx = names % members + jnp.where(late, members, 0)
    segment = lax.axis_index("grp") // SEGMENT
    idx = idx.reshape(-1)
    near_idx = lax.dynamic_slice_in_dim(idx, segment * SEGMENT * listed, SEGMENT * listed, 0)

    tile = edge_tile[0]
    col = edge_col[0]
    tall = 2 * SUB
    far_tile = jnp.where(tile < per_part, tile, tile - per_part)
    is_own = (tile >= per_part) & (tile < 2 * per_part)
    own_key = (col // tall * per_part + tile - per_part) * tall
    far_key = per_part * rows + (col // tall * 2 * per_part + far_tile) * tall
    key = jnp.where(is_own, own_key, far_key) + col % tall
    slab = build_slab(edge_row[0], key, rows, listed * rows)

    chosen_own = select_own(near_idx, own, per_part)
    window_own = segment_swap(chosen_own, members)
    window_far = segment_swap(select_far(near_idx, first, second, per_part), members)
    hidden, partial, grad = layer(
        slab,
        window_own.reshape(rows // tall * per_part, 2, tall, LANE),
        window_far.reshape(rows // tall * 2 * per_part, 2, tall, LANE),
        weight,
        dinv,
        bias[None, :],
        cotangent,
        members,
        listed,
    )
    mine = segment_swap(partial, members)
    grad = swap(grad, "grp")
    share = grad.astype(jnp.float32).sum(axis=0)
    share = swap(jnp.broadcast_to(share[None], (rings, 3, SUB, LANE)), "rep")
    to_first, to_second = collect(near_idx, (0, 2), mine, members, per_part, jnp.bfloat16)
    from_first = with_partner(to_first, "rep")
    from_second = with_other(to_second, "rep")
    (own_sum,) = collect(near_idx, (1,), mine, members, per_part, jnp.float32)

    final, grad_bias = join(own_sum, from_first, from_second, share)
    final = swap(final, "grp")
    grad_features, grad_weight = finish(final, dinv, weight)
    return (hidden, grad_features, grad_weight, grad_bias[0])


def solution(mesh):
    return jax.shard_map(
        per_device,
        mesh=mesh,
        in_specs=(
            P(("rep", "grp"), None),
            P(),
            P(),
            P(("rep", "grp"), None),
            P(("rep", "grp")),
            P(("rep", "grp"), None),
            P(("rep", "grp"), None),
            P(("rep", "grp"), None),
            P(("rep", "grp"), None),
        ),
        out_specs=(P(("rep", "grp"), None), P(("rep", "grp"), None), P(), P()),
        check_vma=False,
    )
```

```python
import functools

import jax
import jax.numpy as jnp
from jax import lax
from jax.experimental import pallas as pl
from jax.experimental.pallas import tpu as pltpu
from jax.sharding import PartitionSpec as P


SUB = 8
LANE = 128
SEGMENT = 8
MIB = 1 << 20


def with_partner(x, axis):
    return lax.ppermute(x, axis, [(i, i ^ 1) for i in range(lax.axis_size(axis))])


def with_other(x, axis):
    size = lax.axis_size(axis)
    return lax.ppermute(x, axis, [(i, (i + 1 if i % 2 else i - 1) % size) for i in range(size)])


def vmem():
    return pl.BlockSpec(memory_space=pltpu.VMEM)


def smem():
    return pl.BlockSpec(memory_space=pltpu.SMEM)


def hbm():
    return pl.BlockSpec(memory_space=pltpu.HBM)


def call(kernel, mib, out_shape, in_specs, out_specs, scratch=()):
    return pl.pallas_call(
        kernel,
        out_shape=out_shape,
        in_specs=in_specs,
        out_specs=out_specs,
        scratch_shapes=list(scratch),
        compiler_params=pltpu.CompilerParams(vmem_limit_bytes=mib * MIB),
    )


def cut_kernel(x_ref, degree_ref, cols_ref, out_ref, dinv_ref, names_ref):
    rows = x_ref.shape[0]
    groups = rows // SUB
    square = (rows, rows)
    diagonal = lax.broadcasted_iota(jnp.int32, square, 0) == lax.broadcasted_iota(jnp.int32, square, 1)
    degree = jnp.sum(jnp.where(diagonal, degree_ref[...].astype(jnp.float32), 0.0), axis=1, keepdims=True)
    dinv = lax.rsqrt(degree)
    dinv_ref[...] = dinv
    names_ref[...] = jnp.zeros_like(names_ref)
    names_ref[:, pl.ds(0, cols_ref.shape[1])] = cols_ref[...].astype(jnp.float32)
    lane = lax.broadcasted_iota(jnp.int32, (rows, LANE), 1)
    note = jnp.where(lane < LANE // 2, names_ref[...], degree).reshape(groups, SUB, LANE).astype(jnp.bfloat16)
    members = out_ref.shape[0]
    for half in range(2):
        scaled = x_ref[:, half * LANE : (half + 1) * LANE].astype(jnp.float32) * dinv
        scaled = scaled.reshape(groups, SUB, LANE).astype(jnp.bfloat16)
        for q in range(members):
            for sub in range(2):
                out_ref[q, 2 * half + sub] = scaled[2 * (q % SEGMENT) + sub]
        for a in range(groups):
            out_ref[half * groups + a, 4] = note[a]


def cut(features, degree, cols):
    rows = features.shape[0]
    return call(
        cut_kernel,
        60,
        (
            jax.ShapeDtypeStruct((2 * rows // SUB, 5, SUB, LANE), jnp.bfloat16),
            jax.ShapeDtypeStruct((rows, 1), jnp.float32),
        ),
        [vmem()] * 3,
        (vmem(), vmem()),
        [pltpu.VMEM((1, LANE), jnp.float32)],
    )(features, degree, cols)


def count_kernel(chunk, xk_ref, yk_ref, out_ref, acc_ref):
    edges = xk_ref.shape[1]
    tall = acc_ref.shape[0]
    wide = acc_ref.shape[1]
    for step in range(edges // chunk):
        xk = xk_ref[:, pl.ds(step * chunk, chunk)]
        yk = yk_ref[:, pl.ds(step * chunk, chunk)]
        left = (lax.broadcasted_iota(jnp.int32, (tall, chunk), 0) == xk).astype(jnp.float32).astype(jnp.bfloat16)
        right = (lax.broadcasted_iota(jnp.int32, (wide, chunk), 0) == yk).astype(jnp.float32).astype(jnp.bfloat16)
        part = lax.dot_general(left, right, (((1,), (1,)), ((), ())), preferred_element_type=jnp.float32)
        if step == 0:
            acc_ref[...] = part
        else:
            acc_ref[...] += part
    rows = out_ref.shape[0]
    for block in range(tall // rows):
        out_ref[:, pl.ds(block * wide, wide)] = acc_ref[pl.ds(block * rows, rows), :].astype(jnp.bfloat16)


def build_slab(row, key, rows, keys):
    wide = 256
    edges = row.shape[0]
    chunk = 768 if edges % 768 == 0 else 128
    tall = rows * (keys // wide)
    xk = ((key // wide) * rows + row).reshape(1, edges)
    yk = (key % wide).reshape(1, edges)
    return pl.pallas_call(
        functools.partial(count_kernel, chunk),
        out_shape=jax.ShapeDtypeStruct((rows, keys), jnp.bfloat16),
        in_specs=[vmem(), vmem()],
        out_specs=vmem(),
        scratch_shapes=[pltpu.VMEM((tall, wide), jnp.float32)],
        compiler_params=pltpu.CompilerParams(vmem_limit_bytes=24 * MIB),
        name="count",
    )(xk, yk)


def select_own_kernel(per_part, idx_ref, own_ref, out_ref, made_ref, sem):
    members = own_ref.shape[0]
    for d in range(SEGMENT):
        for t in range(per_part):
            at = jnp.bitwise_and(idx_ref[d * 3 * per_part + per_part + t], members - 1)
            made_ref[d, t] = own_ref[at]
    copy = pltpu.make_async_copy(made_ref, out_ref, sem)
    copy.start()
    copy.wait()


def select_own(idx, own, per_part):
    shape = (SEGMENT, per_part) + own.shape[1:]
    return call(
        functools.partial(select_own_kernel, per_part),
        6,
        jax.ShapeDtypeStruct(shape, own.dtype),
        [smem(), vmem()],
        hbm(),
        [pltpu.VMEM(shape, own.dtype), pltpu.SemaphoreType.DMA],
    )(idx, own)


def select_far_kernel(per_part, idx_ref, first_ref, second_ref, out_ref, near_ref):
    members = first_ref.shape[0]
    near_ref[pl.ds(0, members)] = first_ref[...]
    near_ref[pl.ds(members, members)] = second_ref[...]
    for d in range(SEGMENT):
        for t in range(2 * per_part):
            place = t if t < per_part else t + per_part
            at = jnp.bitwise_and(idx_ref[d * 3 * per_part + place], 2 * members - 1)
            out_ref[d, t] = near_ref[at]


def select_far(idx, first, second, per_part):
    members = first.shape[0]
    return call(
        functools.partial(select_far_kernel, per_part),
        6,
        jax.ShapeDtypeStruct((SEGMENT, 2 * per_part) + first.shape[1:], first.dtype),
        [smem(), vmem(), vmem()],
        vmem(),
        [pltpu.VMEM((2 * members,) + first.shape[1:], first.dtype)],
    )(idx, first, second)


def layer_kernel(listed, slab_ref, xown_ref, xfar_ref, weight_ref, dinv_ref, bias_ref, cot_ref, hid_ref, part_ref):
    dinv = dinv_ref[...]
    per_part = listed // 3
    tall = 2 * SUB
    edge = xown_ref.shape[0] * tall
    rows = []
    for half in range(2):
        near = xown_ref[:, half].reshape(edge, LANE)
        far = xfar_ref[:, half].reshape(2 * edge, LANE)
        total = jnp.dot(slab_ref[:, :edge], near, preferred_element_type=jnp.float32)
        rows.append(total + jnp.dot(slab_ref[:, edge:], far, preferred_element_type=jnp.float32))
    gathered = jnp.concatenate(rows, axis=1)
    high = gathered.astype(jnp.bfloat16)
    low = (gathered - high.astype(jnp.float32)).astype(jnp.bfloat16)
    weight = weight_ref[...]
    total = jnp.dot(high, weight, preferred_element_type=jnp.float32)
    total = total + jnp.dot(low, weight, preferred_element_type=jnp.float32)
    pre = total * dinv + bias_ref[...]
    sig = jax.nn.sigmoid(pre)
    hid_ref[...] = (pre * sig).astype(hid_ref.dtype)
    grad_pre = cot_ref[...].astype(jnp.float32) * sig * (1.0 + pre * (1.0 - sig))
    back = (grad_pre * dinv).astype(jnp.bfloat16)
    contract = (((0,), (0,)), ((), ()))
    grad = lax.dot_general(high, back, contract, preferred_element_type=jnp.float32)
    grad = grad + lax.dot_general(low, back, contract, preferred_element_type=jnp.float32)
    sums = jnp.sum(grad_pre, axis=0, keepdims=True)
    sums_high = sums.astype(jnp.bfloat16).astype(jnp.float32)
    sums_low = sums - sums_high
    at = lax.broadcasted_iota(jnp.int32, (SUB, LANE), 0)
    extra = jnp.zeros((SUB, LANE), jnp.float32)
    for index, value in enumerate((sums_high, sums_low)):
        for half in range(2):
            lanes = slice(half * LANE, (half + 1) * LANE)
            extra = jnp.where(at == 2 * index + half, value[:, lanes], extra)
    extra = extra.astype(jnp.bfloat16)
    segments = grad.shape[0] // (SUB * SEGMENT)
    for half in range(2):
        lanes = slice(half * LANE, (half + 1) * LANE)
        partial = lax.dot_general(slab_ref[...], back[:, lanes], contract, preferred_element_type=jnp.float32)
        for holder in range(SEGMENT):
            at = holder * per_part * tall
            near = partial[at : at + per_part * tall].reshape(per_part, 2, SUB, LANE).astype(jnp.bfloat16)
            at = edge + 2 * at
            far = partial[at : at + 2 * per_part * tall].reshape(2 * per_part, 2, SUB, LANE).astype(jnp.bfloat16)
            for t in range(per_part):
                part_ref[holder, pl.ds(4 * t + 2 * half, 2)] = far[t]
                part_ref[holder, pl.ds(4 * (per_part + t) + 2 * half, 2)] = near[t]
                part_ref[holder, pl.ds(4 * (2 * per_part + t) + 2 * half, 2)] = far[per_part + t]
            part_ref[holder, 4 * listed] = extra
            for segment in range(segments):
                top = (segment * SEGMENT + holder) * SUB
                block = grad[top : top + SUB, lanes]
                part_ref[holder, 4 * listed + 1 + 2 * segment + half] = block.astype(jnp.bfloat16)


def layer(slab, xown, xfar, weight, dinv, bias, cotangent, listed):
    rows, width = cotangent.shape
    pieces = 4 * listed + 1 + 2 * (width // (SUB * SEGMENT))
    return call(
        functools.partial(layer_kernel, listed),
        16,
        (
            jax.ShapeDtypeStruct((rows, width), jnp.bfloat16),
            jax.ShapeDtypeStruct((SEGMENT, pieces, SUB, LANE), jnp.bfloat16),
        ),
        [vmem()] * 7,
        (vmem(), vmem()),
    )(slab, xown, xfar, weight, dinv, bias, cotangent)


def fold_kernel(got_ref, out_ref, made_ref, sem):
    segments = made_ref.shape[0]
    first = got_ref.shape[1] - 1 - 2 * segments
    total = got_ref[0, pl.ds(first, 1 + 2 * segments)].astype(jnp.float32)
    for d in range(1, got_ref.shape[0]):
        total = total + got_ref[d, pl.ds(first, 1 + 2 * segments)].astype(jnp.float32)
    for segment in range(segments):
        made_ref[segment, 0] = total[0]
        made_ref[segment, 1] = total[1 + 2 * segment]
        made_ref[segment, 2] = total[2 + 2 * segment]
    copy = pltpu.make_async_copy(made_ref, out_ref, sem)
    copy.start()
    copy.wait()


def fold(got, segments):
    shape = (segments, 3, SUB, LANE)
    return call(
        fold_kernel,
        4,
        jax.ShapeDtypeStruct(shape, jnp.float32),
        [vmem()],
        hbm(),
        [pltpu.VMEM(shape, jnp.float32), pltpu.SemaphoreType.DMA],
    )(got)


def collect_kernel(members, per_part, parts, chains, idx_ref, got_ref, *refs):
    outs, acc_ref = refs[:-1], refs[-1]
    acc_ref[...] = jnp.zeros_like(acc_ref)
    tiles = acc_ref.shape[1]
    for step in range(SEGMENT // chains):
        for part in parts:
            for t in range(part * per_part, (part + 1) * per_part):
                for j in range(chains):
                    d = step * chains + j
                    at = jnp.bitwise_and(idx_ref[d * 3 * per_part + t], tiles - 1)
                    acc_ref[j, at] += got_ref[d, pl.ds(4 * t, 4)].astype(jnp.float32)
    for number, ref in enumerate(outs):
        part = pl.ds(number * members, members)
        value = acc_ref[0, part]
        for j in range(1, chains):
            value = value + acc_ref[j, part]
        ref[...] = value.astype(ref.dtype)


def collect(idx, parts, got, members, per_part, dtype):
    chains = 2
    piece = (members, 4, SUB, LANE)
    return call(
        functools.partial(collect_kernel, members, per_part, parts, chains),
        8,
        tuple(jax.ShapeDtypeStruct(piece, dtype) for _ in parts),
        [smem(), vmem()],
        (vmem(),) * len(parts),
        [pltpu.VMEM((chains, len(parts) * members, 4, SUB, LANE), jnp.float32)],
    )(idx, got)


def join_kernel(own_ref, first_ref, second_ref, share_ref, out_ref, bias_ref):
    members = own_ref.shape[0]
    total = share_ref[0]
    for ring in range(1, share_ref.shape[0]):
        total = total + share_ref[ring]
    for half in range(2):
        bias_ref[:, half * LANE : (half + 1) * LANE] = total[0, half : half + 1] + total[0, half + 2 : half + 3]
    rows = [total[1].astype(jnp.bfloat16), total[2].astype(jnp.bfloat16)]
    for m in range(members):
        grad = own_ref[m] + first_ref[m].astype(jnp.float32) + second_ref[m].astype(jnp.float32)
        out_ref[m, pl.ds(0, 4)] = grad.astype(jnp.bfloat16)
        out_ref[m, 4] = rows[0]
        out_ref[m, 5] = rows[1]


def join(own, first, second, share):
    members = own.shape[0]
    return call(
        join_kernel,
        6,
        (
            jax.ShapeDtypeStruct((members, 6, SUB, LANE), jnp.bfloat16),
            jax.ShapeDtypeStruct((1, 2 * LANE), jnp.float32),
        ),
        [vmem()] * 4,
        (vmem(), vmem()),
    )(own, first, second, share)


def finish_kernel(final_ref, dinv_ref, weight_ref, features_ref, weight_grad_ref):
    members = final_ref.shape[0]
    dinv = dinv_ref[...]
    sides = []
    for half in range(2):
        pair = pl.ds(2 * half, 2)
        total = final_ref[pl.ds(0, SEGMENT), pair].astype(jnp.float32)
        for first in range(SEGMENT, members, SEGMENT):
            total = total + final_ref[pl.ds(first, SEGMENT), pair].astype(jnp.float32)
        sides.append(total.reshape(-1, LANE) * dinv)
    grad = jnp.concatenate(sides, axis=1).astype(jnp.bfloat16)
    features_ref[...] = lax.dot_general(
        grad, weight_ref[...], (((1,), (1,)), ((), ())), preferred_element_type=jnp.float32
    ).astype(features_ref.dtype)
    for half in range(2):
        rows = final_ref[:, 4 + half].astype(jnp.float32).reshape(-1, LANE)
        weight_grad_ref[:, half * LANE : (half + 1) * LANE] = rows


def finish(final, dinv, weight):
    width = weight.shape[0]
    rows = dinv.shape[0]
    return call(
        finish_kernel,
        6,
        (
            jax.ShapeDtypeStruct((rows, width), jnp.bfloat16),
            jax.ShapeDtypeStruct((width, width), jnp.float32),
        ),
        [vmem()] * 3,
        (vmem(), vmem()),
    )(final, dinv, weight)


def swap(x, axis):
    return lax.all_to_all(x, axis, 0, 0, tiled=True)


def segment_swap(x, members):
    groups = [list(range(first, first + SEGMENT)) for first in range(0, members, SEGMENT)]
    return lax.all_to_all(x, "grp", 0, 0, axis_index_groups=groups, tiled=True)


def across_swap(x, members):
    groups = [list(range(first, members, SEGMENT)) for first in range(SEGMENT)]
    return lax.all_to_all(x, "grp", 0, 0, axis_index_groups=groups, tiled=True)


def per_device(features, weight, bias, cotangent, degree, tile_cols, edge_tile, edge_row, edge_col):
    rows, _ = features.shape
    members = lax.axis_size("grp")
    rings = lax.axis_size("rep")
    listed = tile_cols.shape[1]
    per_part = listed // 3

    payload, dinv = cut(features, degree[None, :], tile_cols)
    got = swap(payload, "grp")
    own = got[:, :4]
    first = with_partner(own, "rep")
    second = with_other(own, "rep")

    names = got[:, 4, 0, :listed].astype(jnp.int32)
    part = lax.broadcasted_iota(jnp.int32, names.shape, 1) // per_part
    even = lax.axis_index("rep") % 2 == 0
    late = jnp.where(even, part == 0, part == 2)
    idx = names % members + jnp.where(late, members, 0)
    segment = lax.axis_index("grp") // SEGMENT
    idx = idx.reshape(-1)
    near_idx = lax.dynamic_slice_in_dim(idx, segment * SEGMENT * listed, SEGMENT * listed, 0)

    tile = edge_tile[0]
    col = edge_col[0]
    tall = 2 * SUB
    far_tile = jnp.where(tile < per_part, tile, tile - per_part)
    is_own = (tile >= per_part) & (tile < 2 * per_part)
    own_key = (col // tall * per_part + tile - per_part) * tall
    far_key = per_part * rows + (col // tall * 2 * per_part + far_tile) * tall
    key = jnp.where(is_own, own_key, far_key) + col % tall
    slab = build_slab(edge_row[0], key, rows, listed * rows)

    chosen_own = select_own(near_idx, own, per_part)
    window_own = segment_swap(chosen_own, members)
    window_far = segment_swap(select_far(near_idx, first, second, per_part), members)
    hidden, partial = layer(
        slab,
        window_own.reshape(rows // tall * per_part, 2, tall, LANE),
        window_far.reshape(rows // tall * 2 * per_part, 2, tall, LANE),
        weight,
        dinv,
        bias[None, :],
        cotangent,
        listed,
    )
    mine = segment_swap(partial, members)
    grad = across_swap(fold(mine, members // SEGMENT), members)
    share = grad.sum(axis=0)
    share = swap(jnp.broadcast_to(share[None], (rings, 3, SUB, LANE)), "rep")
    to_first, to_second = collect(near_idx, (0, 2), mine, members, per_part, jnp.bfloat16)
    from_first = with_partner(to_first, "rep")
    from_second = with_other(to_second, "rep")
    (own_sum,) = collect(near_idx, (1,), mine, members, per_part, jnp.float32)

    final, grad_bias = join(own_sum, from_first, from_second, share)
    final = swap(final, "grp")
    grad_features, grad_weight = finish(final, dinv, weight)
    return (hidden, grad_features, grad_weight, grad_bias[0])


def solution(mesh):
    return jax.shard_map(
        per_device,
        mesh=mesh,
        in_specs=(
            P(("rep", "grp"), None),
            P(),
            P(),
            P(("rep", "grp"), None),
            P(("rep", "grp")),
            P(("rep", "grp"), None),
            P(("rep", "grp"), None),
            P(("rep", "grp"), None),
            P(("rep", "grp"), None),
        ),
        out_specs=(P(("rep", "grp"), None), P(("rep", "grp"), None), P(), P()),
        check_vma=False,
    )
```

```python
import functools

import jax
import jax.numpy as jnp
from jax import lax
from jax.experimental import pallas as pl
from jax.experimental.pallas import tpu as pltpu
from jax.sharding import PartitionSpec as P


SUB = 8
LANE = 128
SEGMENT = 8
MIB = 1 << 20


def with_partner(x, axis):
    return lax.ppermute(x, axis, [(i, i ^ 1) for i in range(lax.axis_size(axis))])


def with_other(x, axis):
    size = lax.axis_size(axis)
    return lax.ppermute(x, axis, [(i, (i + 1 if i % 2 else i - 1) % size) for i in range(size)])


def vmem():
    return pl.BlockSpec(memory_space=pltpu.VMEM)


def smem():
    return pl.BlockSpec(memory_space=pltpu.SMEM)


def hbm():
    return pl.BlockSpec(memory_space=pltpu.HBM)


def call(kernel, mib, out_shape, in_specs, out_specs, scratch=()):
    return pl.pallas_call(
        kernel,
        out_shape=out_shape,
        in_specs=in_specs,
        out_specs=out_specs,
        scratch_shapes=list(scratch),
        compiler_params=pltpu.CompilerParams(vmem_limit_bytes=mib * MIB),
    )


def cut_kernel(x_ref, degree_ref, cols_ref, out_ref, dinv_ref, names_ref):
    rows = x_ref.shape[0]
    groups = rows // SUB
    square = (rows, rows)
    diagonal = lax.broadcasted_iota(jnp.int32, square, 0) == lax.broadcasted_iota(jnp.int32, square, 1)
    degree = jnp.sum(jnp.where(diagonal, degree_ref[...].astype(jnp.float32), 0.0), axis=1, keepdims=True)
    dinv = lax.rsqrt(degree)
    dinv_ref[...] = dinv
    names_ref[...] = jnp.zeros_like(names_ref)
    names_ref[:, pl.ds(0, cols_ref.shape[1])] = cols_ref[...].astype(jnp.float32)
    lane = lax.broadcasted_iota(jnp.int32, (rows, LANE), 1)
    note = jnp.where(lane < LANE // 2, names_ref[...], degree).reshape(groups, SUB, LANE).astype(jnp.bfloat16)
    members = out_ref.shape[0]
    for half in range(2):
        scaled = x_ref[:, half * LANE : (half + 1) * LANE].astype(jnp.float32) * dinv
        scaled = scaled.reshape(groups, SUB, LANE).astype(jnp.bfloat16)
        for q in range(members):
            for sub in range(2):
                out_ref[q, 2 * half + sub] = scaled[2 * (q % SEGMENT) + sub]
        for a in range(groups):
            out_ref[half * groups + a, 4] = note[a]


def cut(features, degree, cols):
    rows = features.shape[0]
    return call(
        cut_kernel,
        60,
        (
            jax.ShapeDtypeStruct((2 * rows // SUB, 5, SUB, LANE), jnp.bfloat16),
            jax.ShapeDtypeStruct((rows, 1), jnp.float32),
        ),
        [vmem()] * 3,
        (vmem(), vmem()),
        [pltpu.VMEM((1, LANE), jnp.float32)],
    )(features, degree, cols)


def count_kernel(chunk, xk_ref, yk_ref, out_ref, acc_ref):
    edges = xk_ref.shape[1]
    tall = acc_ref.shape[0]
    wide = acc_ref.shape[1]
    for step in range(edges // chunk):
        xk = xk_ref[:, pl.ds(step * chunk, chunk)]
        yk = yk_ref[:, pl.ds(step * chunk, chunk)]
        left = (lax.broadcasted_iota(jnp.int32, (tall, chunk), 0) == xk).astype(jnp.float32).astype(jnp.bfloat16)
        right = (lax.broadcasted_iota(jnp.int32, (wide, chunk), 0) == yk).astype(jnp.float32).astype(jnp.bfloat16)
        part = lax.dot_general(left, right, (((1,), (1,)), ((), ())), preferred_element_type=jnp.float32)
        if step == 0:
            acc_ref[...] = part
        else:
            acc_ref[...] += part
    rows = out_ref.shape[0]
    for block in range(tall // rows):
        out_ref[:, pl.ds(block * wide, wide)] = acc_ref[pl.ds(block * rows, rows), :].astype(jnp.bfloat16)


def build_slab(row, key, rows, keys):
    wide = 256
    edges = row.shape[0]
    chunk = 768 if edges % 768 == 0 else 128
    tall = rows * (keys // wide)
    xk = ((key // wide) * rows + row).reshape(1, edges)
    yk = (key % wide).reshape(1, edges)
    return pl.pallas_call(
        functools.partial(count_kernel, chunk),
        out_shape=jax.ShapeDtypeStruct((rows, keys), jnp.bfloat16),
        in_specs=[vmem(), vmem()],
        out_specs=vmem(),
        scratch_shapes=[pltpu.VMEM((tall, wide), jnp.float32)],
        compiler_params=pltpu.CompilerParams(vmem_limit_bytes=24 * MIB),
        name="count",
    )(xk, yk)


def select_own_kernel(per_part, idx_ref, own_ref, out_ref, made_ref, sem):
    members = own_ref.shape[0]
    for d in range(SEGMENT):
        for t in range(per_part):
            at = jnp.bitwise_and(idx_ref[d * 3 * per_part + per_part + t], members - 1)
            made_ref[d, t] = own_ref[at]
    copy = pltpu.make_async_copy(made_ref, out_ref, sem)
    copy.start()
    copy.wait()


def select_own(idx, own, per_part):
    shape = (SEGMENT, per_part) + own.shape[1:]
    return call(
        functools.partial(select_own_kernel, per_part),
        6,
        jax.ShapeDtypeStruct(shape, own.dtype),
        [smem(), vmem()],
        hbm(),
        [pltpu.VMEM(shape, own.dtype), pltpu.SemaphoreType.DMA],
    )(idx, own)


def select_far_kernel(per_part, idx_ref, first_ref, second_ref, out_ref, near_ref):
    members = first_ref.shape[0]
    near_ref[pl.ds(0, members)] = first_ref[...]
    near_ref[pl.ds(members, members)] = second_ref[...]
    for d in range(SEGMENT):
        for t in range(2 * per_part):
            place = t if t < per_part else t + per_part
            at = jnp.bitwise_and(idx_ref[d * 3 * per_part + place], 2 * members - 1)
            out_ref[d, t] = near_ref[at]


def select_far(idx, first, second, per_part):
    members = first.shape[0]
    return call(
        functools.partial(select_far_kernel, per_part),
        6,
        jax.ShapeDtypeStruct((SEGMENT, 2 * per_part) + first.shape[1:], first.dtype),
        [smem(), vmem(), vmem()],
        vmem(),
        [pltpu.VMEM((2 * members,) + first.shape[1:], first.dtype)],
    )(idx, first, second)


def layer_kernel(listed, slab_ref, xown_ref, xfar_ref, weight_ref, dinv_ref, bias_ref, cot_ref, hid_ref, part_ref):
    dinv = dinv_ref[...]
    per_part = listed // 3
    tall = 2 * SUB
    edge = xown_ref.shape[0] * tall
    rows = []
    for half in range(2):
        near = xown_ref[:, half].reshape(edge, LANE)
        far = xfar_ref[:, half].reshape(2 * edge, LANE)
        total = jnp.dot(slab_ref[:, :edge], near, preferred_element_type=jnp.float32)
        rows.append(total + jnp.dot(slab_ref[:, edge:], far, preferred_element_type=jnp.float32))
    gathered = jnp.concatenate(rows, axis=1)
    high = gathered.astype(jnp.bfloat16)
    low = (gathered - high.astype(jnp.float32)).astype(jnp.bfloat16)
    weight = weight_ref[...]
    total = jnp.dot(high, weight, preferred_element_type=jnp.float32)
    total = total + jnp.dot(low, weight, preferred_element_type=jnp.float32)
    pre = total * dinv + bias_ref[...]
    sig = jax.nn.sigmoid(pre)
    hid_ref[...] = (pre * sig).astype(hid_ref.dtype)
    grad_pre = cot_ref[...].astype(jnp.float32) * sig * (1.0 + pre * (1.0 - sig))
    back = (grad_pre * dinv).astype(jnp.bfloat16)
    contract = (((0,), (0,)), ((), ()))
    grad = lax.dot_general(high, back, contract, preferred_element_type=jnp.float32)
    grad = grad + lax.dot_general(low, back, contract, preferred_element_type=jnp.float32)
    sums = jnp.sum(grad_pre, axis=0, keepdims=True)
    sums_high = sums.astype(jnp.bfloat16).astype(jnp.float32)
    sums_low = sums - sums_high
    at = lax.broadcasted_iota(jnp.int32, (SUB, LANE), 0)
    extra = jnp.zeros((SUB, LANE), jnp.float32)
    for index, value in enumerate((sums_high, sums_low)):
        for half in range(2):
            lanes = slice(half * LANE, (half + 1) * LANE)
            extra = jnp.where(at == 2 * index + half, value[:, lanes], extra)
    extra = extra.astype(jnp.bfloat16)
    segments = grad.shape[0] // (SUB * SEGMENT)
    for half in range(2):
        lanes = slice(half * LANE, (half + 1) * LANE)
        partial = lax.dot_general(slab_ref[...], back[:, lanes], contract, preferred_element_type=jnp.float32)
        for holder in range(SEGMENT):
            at = holder * per_part * tall
            near = partial[at : at + per_part * tall].reshape(per_part, 2, SUB, LANE).astype(jnp.bfloat16)
            at = edge + 2 * at
            far = partial[at : at + 2 * per_part * tall].reshape(2 * per_part, 2, SUB, LANE).astype(jnp.bfloat16)
            for t in range(per_part):
                part_ref[holder, pl.ds(4 * t + 2 * half, 2)] = far[t]
                part_ref[holder, pl.ds(4 * (per_part + t) + 2 * half, 2)] = near[t]
                part_ref[holder, pl.ds(4 * (2 * per_part + t) + 2 * half, 2)] = far[per_part + t]
            part_ref[holder, 4 * listed] = extra
            for segment in range(segments):
                top = (segment * SEGMENT + holder) * SUB
                block = grad[top : top + SUB, lanes]
                part_ref[holder, 4 * listed + 1 + 2 * segment + half] = block.astype(jnp.bfloat16)


def layer(slab, xown, xfar, weight, dinv, bias, cotangent, listed):
    rows, width = cotangent.shape
    pieces = 4 * listed + 1 + 2 * (width // (SUB * SEGMENT))
    return call(
        functools.partial(layer_kernel, listed),
        16,
        (
            jax.ShapeDtypeStruct((rows, width), jnp.bfloat16),
            jax.ShapeDtypeStruct((SEGMENT, pieces, SUB, LANE), jnp.bfloat16),
        ),
        [vmem()] * 7,
        (vmem(), vmem()),
    )(slab, xown, xfar, weight, dinv, bias, cotangent)


def fold_kernel(got_ref, out_ref, made_ref, sem):
    segments = made_ref.shape[0]
    first = got_ref.shape[1] - 1 - 2 * segments
    total = got_ref[0, pl.ds(first, 1 + 2 * segments)].astype(jnp.float32)
    for d in range(1, got_ref.shape[0]):
        total = total + got_ref[d, pl.ds(first, 1 + 2 * segments)].astype(jnp.float32)
    for segment in range(segments):
        made_ref[segment, 0] = total[0]
        made_ref[segment, 1] = total[1 + 2 * segment]
        made_ref[segment, 2] = total[2 + 2 * segment]
    copy = pltpu.make_async_copy(made_ref, out_ref, sem)
    copy.start()
    copy.wait()


def fold(got, segments):
    shape = (segments, 3, SUB, LANE)
    return call(
        fold_kernel,
        4,
        jax.ShapeDtypeStruct(shape, jnp.float32),
        [vmem()],
        hbm(),
        [pltpu.VMEM(shape, jnp.float32), pltpu.SemaphoreType.DMA],
    )(got)


def spread_kernel(got_ref, out_ref, made_ref, sem):
    total = got_ref[0]
    for segment in range(1, got_ref.shape[0]):
        total = total + got_ref[segment]
    top = total[0, 0:2] + total[0, 2:4]
    high = top.astype(jnp.bfloat16).astype(jnp.float32)
    low = top - high
    at = lax.broadcasted_iota(jnp.int32, (SUB, LANE), 0)
    piece = jnp.zeros((SUB, LANE), jnp.float32)
    for index in range(2):
        piece = jnp.where(at == index, high[index : index + 1], piece)
        piece = jnp.where(at == 2 + index, low[index : index + 1], piece)
    pieces = [piece.astype(jnp.bfloat16), total[1].astype(jnp.bfloat16), total[2].astype(jnp.bfloat16)]
    for ring in range(made_ref.shape[0]):
        for number, value in enumerate(pieces):
            made_ref[ring, number] = value
    copy = pltpu.make_async_copy(made_ref, out_ref, sem)
    copy.start()
    copy.wait()


def spread(got, rings):
    shape = (rings, 3, SUB, LANE)
    return call(
        spread_kernel,
        4,
        jax.ShapeDtypeStruct(shape, jnp.bfloat16),
        [vmem()],
        hbm(),
        [pltpu.VMEM(shape, jnp.bfloat16), pltpu.SemaphoreType.DMA],
    )(got)


def collect_kernel(members, per_part, parts, chains, idx_ref, got_ref, *refs):
    outs, acc_ref = refs[:-1], refs[-1]
    acc_ref[...] = jnp.zeros_like(acc_ref)
    tiles = acc_ref.shape[1]
    for step in range(SEGMENT // chains):
        for part in parts:
            for t in range(part * per_part, (part + 1) * per_part):
                for j in range(chains):
                    d = step * chains + j
                    at = jnp.bitwise_and(idx_ref[d * 3 * per_part + t], tiles - 1)
                    acc_ref[j, at] += got_ref[d, pl.ds(4 * t, 4)].astype(jnp.float32)
    for number, ref in enumerate(outs):
        part = pl.ds(number * members, members)
        value = acc_ref[0, part]
        for j in range(1, chains):
            value = value + acc_ref[j, part]
        ref[...] = value.astype(ref.dtype)


def collect(idx, parts, got, members, per_part, dtype):
    chains = 2
    piece = (members, 4, SUB, LANE)
    return call(
        functools.partial(collect_kernel, members, per_part, parts, chains),
        8,
        tuple(jax.ShapeDtypeStruct(piece, dtype) for _ in parts),
        [smem(), vmem()],
        (vmem(),) * len(parts),
        [pltpu.VMEM((chains, len(parts) * members, 4, SUB, LANE), jnp.float32)],
    )(idx, got)


def join_kernel(own_ref, first_ref, second_ref, share_ref, out_ref, bias_ref):
    members = own_ref.shape[0]
    total = share_ref[0].astype(jnp.float32)
    for ring in range(1, share_ref.shape[0]):
        total = total + share_ref[ring].astype(jnp.float32)
    for half in range(2):
        bias_ref[:, half * LANE : (half + 1) * LANE] = total[0, half : half + 1] + total[0, half + 2 : half + 3]
    rows = [total[1].astype(jnp.bfloat16), total[2].astype(jnp.bfloat16)]
    for m in range(members):
        grad = own_ref[m] + first_ref[m].astype(jnp.float32) + second_ref[m].astype(jnp.float32)
        out_ref[m, pl.ds(0, 4)] = grad.astype(jnp.bfloat16)
        out_ref[m, 4] = rows[0]
        out_ref[m, 5] = rows[1]


def join(own, first, second, share):
    members = own.shape[0]
    return call(
        join_kernel,
        6,
        (
            jax.ShapeDtypeStruct((members, 6, SUB, LANE), jnp.bfloat16),
            jax.ShapeDtypeStruct((1, 2 * LANE), jnp.float32),
        ),
        [vmem()] * 4,
        (vmem(), vmem()),
    )(own, first, second, share)


def finish_kernel(final_ref, dinv_ref, weight_ref, features_ref, weight_grad_ref):
    members = final_ref.shape[0]
    dinv = dinv_ref[...]
    sides = []
    for half in range(2):
        pair = pl.ds(2 * half, 2)
        total = final_ref[pl.ds(0, SEGMENT), pair].astype(jnp.float32)
        for first in range(SEGMENT, members, SEGMENT):
            total = total + final_ref[pl.ds(first, SEGMENT), pair].astype(jnp.float32)
        sides.append(total.reshape(-1, LANE) * dinv)
    grad = jnp.concatenate(sides, axis=1).astype(jnp.bfloat16)
    features_ref[...] = lax.dot_general(
        grad, weight_ref[...], (((1,), (1,)), ((), ())), preferred_element_type=jnp.float32
    ).astype(features_ref.dtype)
    for half in range(2):
        rows = final_ref[:, 4 + half].astype(jnp.float32).reshape(-1, LANE)
        weight_grad_ref[:, half * LANE : (half + 1) * LANE] = rows


def finish(final, dinv, weight):
    width = weight.shape[0]
    rows = dinv.shape[0]
    return call(
        finish_kernel,
        6,
        (
            jax.ShapeDtypeStruct((rows, width), jnp.bfloat16),
            jax.ShapeDtypeStruct((width, width), jnp.float32),
        ),
        [vmem()] * 3,
        (vmem(), vmem()),
    )(final, dinv, weight)


def swap(x, axis):
    return lax.all_to_all(x, axis, 0, 0, tiled=True)


def segment_swap(x, members):
    groups = [list(range(first, first + SEGMENT)) for first in range(0, members, SEGMENT)]
    return lax.all_to_all(x, "grp", 0, 0, axis_index_groups=groups, tiled=True)


def across_swap(x, members):
    groups = [list(range(first, members, SEGMENT)) for first in range(SEGMENT)]
    return lax.all_to_all(x, "grp", 0, 0, axis_index_groups=groups, tiled=True)


def per_device(features, weight, bias, cotangent, degree, tile_cols, edge_tile, edge_row, edge_col):
    rows, _ = features.shape
    members = lax.axis_size("grp")
    rings = lax.axis_size("rep")
    listed = tile_cols.shape[1]
    per_part = listed // 3

    payload, dinv = cut(features, degree[None, :], tile_cols)
    got = swap(payload, "grp")
    own = got[:, :4]
    first = with_partner(own, "rep")
    second = with_other(own, "rep")

    names = got[:, 4, 0, :listed].astype(jnp.int32)
    part = lax.broadcasted_iota(jnp.int32, names.shape, 1) // per_part
    even = lax.axis_index("rep") % 2 == 0
    late = jnp.where(even, part == 0, part == 2)
    idx = names % members + jnp.where(late, members, 0)
    segment = lax.axis_index("grp") // SEGMENT
    idx = idx.reshape(-1)
    near_idx = lax.dynamic_slice_in_dim(idx, segment * SEGMENT * listed, SEGMENT * listed, 0)

    tile = edge_tile[0]
    col = edge_col[0]
    tall = 2 * SUB
    far_tile = jnp.where(tile < per_part, tile, tile - per_part)
    is_own = (tile >= per_part) & (tile < 2 * per_part)
    own_key = (col // tall * per_part + tile - per_part) * tall
    far_key = per_part * rows + (col // tall * 2 * per_part + far_tile) * tall
    key = jnp.where(is_own, own_key, far_key) + col % tall
    slab = build_slab(edge_row[0], key, rows, listed * rows)

    chosen_own = select_own(near_idx, own, per_part)
    window_own = segment_swap(chosen_own, members)
    window_far = segment_swap(select_far(near_idx, first, second, per_part), members)
    hidden, partial = layer(
        slab,
        window_own.reshape(rows // tall * per_part, 2, tall, LANE),
        window_far.reshape(rows // tall * 2 * per_part, 2, tall, LANE),
        weight,
        dinv,
        bias[None, :],
        cotangent,
        listed,
    )
    mine = segment_swap(partial, members)
    grad = across_swap(fold(mine, members // SEGMENT), members)
    share = spread(grad, rings)
    share = swap(share, "rep")
    to_first, to_second = collect(near_idx, (0, 2), mine, members, per_part, jnp.bfloat16)
    from_first = with_partner(to_first, "rep")
    from_second = with_other(to_second, "rep")
    (own_sum,) = collect(near_idx, (1,), mine, members, per_part, jnp.float32)

    final, grad_bias = join(own_sum, from_first, from_second, share)
    final = swap(final, "grp")
    grad_features, grad_weight = finish(final, dinv, weight)
    return (hidden, grad_features, grad_weight, grad_bias[0])


def solution(mesh):
    return jax.shard_map(
        per_device,
        mesh=mesh,
        in_specs=(
            P(("rep", "grp"), None),
            P(),
            P(),
            P(("rep", "grp"), None),
            P(("rep", "grp")),
            P(("rep", "grp"), None),
            P(("rep", "grp"), None),
            P(("rep", "grp"), None),
            P(("rep", "grp"), None),
        ),
        out_specs=(P(("rep", "grp"), None), P(("rep", "grp"), None), P(), P()),
        check_vma=False,
    )
```

```python
import functools

import jax
import jax.numpy as jnp
from jax import lax
from jax.experimental import pallas as pl
from jax.experimental.pallas import tpu as pltpu
from jax.sharding import PartitionSpec as P


SUB = 8
LANE = 128
SEGMENT = 8
MIB = 1 << 20


def with_partner(x, axis):
    return lax.ppermute(x, axis, [(i, i ^ 1) for i in range(lax.axis_size(axis))])


def with_other(x, axis):
    size = lax.axis_size(axis)
    return lax.ppermute(x, axis, [(i, (i + 1 if i % 2 else i - 1) % size) for i in range(size)])


def vmem():
    return pl.BlockSpec(memory_space=pltpu.VMEM)


def smem():
    return pl.BlockSpec(memory_space=pltpu.SMEM)


def hbm():
    return pl.BlockSpec(memory_space=pltpu.HBM)


def call(kernel, mib, out_shape, in_specs, out_specs, scratch=()):
    return pl.pallas_call(
        kernel,
        out_shape=out_shape,
        in_specs=in_specs,
        out_specs=out_specs,
        scratch_shapes=list(scratch),
        compiler_params=pltpu.CompilerParams(vmem_limit_bytes=mib * MIB),
    )


def cut_kernel(x_ref, degree_ref, cols_ref, out_ref, dinv_ref, names_ref):
    rows = x_ref.shape[0]
    groups = rows // SUB
    square = (rows, rows)
    diagonal = lax.broadcasted_iota(jnp.int32, square, 0) == lax.broadcasted_iota(jnp.int32, square, 1)
    degree = jnp.sum(jnp.where(diagonal, degree_ref[...].astype(jnp.float32), 0.0), axis=1, keepdims=True)
    dinv = lax.rsqrt(degree)
    dinv_ref[...] = dinv
    names_ref[...] = jnp.zeros_like(names_ref)
    names_ref[:, pl.ds(0, cols_ref.shape[1])] = cols_ref[...].astype(jnp.float32)
    lane = lax.broadcasted_iota(jnp.int32, (rows, LANE), 1)
    note = jnp.where(lane < LANE // 2, names_ref[...], degree).reshape(groups, SUB, LANE).astype(jnp.bfloat16)
    members = out_ref.shape[0]
    for half in range(2):
        scaled = x_ref[:, half * LANE : (half + 1) * LANE].astype(jnp.float32) * dinv
        scaled = scaled.reshape(groups, SUB, LANE).astype(jnp.bfloat16)
        for q in range(members):
            for sub in range(2):
                out_ref[q, 2 * half + sub] = scaled[2 * (q % SEGMENT) + sub]
        for a in range(groups):
            out_ref[half * groups + a, 4] = note[a]


def cut(features, degree, cols):
    rows = features.shape[0]
    return call(
        cut_kernel,
        60,
        (
            jax.ShapeDtypeStruct((2 * rows // SUB, 5, SUB, LANE), jnp.bfloat16),
            jax.ShapeDtypeStruct((rows, 1), jnp.float32),
        ),
        [vmem()] * 3,
        (vmem(), vmem()),
        [pltpu.VMEM((1, LANE), jnp.float32)],
    )(features, degree, cols)


def count_kernel(chunk, xk_ref, yk_ref, out_ref, acc_ref):
    edges = xk_ref.shape[1]
    tall = acc_ref.shape[0]
    wide = acc_ref.shape[1]
    for step in range(edges // chunk):
        xk = xk_ref[:, pl.ds(step * chunk, chunk)]
        yk = yk_ref[:, pl.ds(step * chunk, chunk)]
        left = (lax.broadcasted_iota(jnp.int32, (tall, chunk), 0) == xk).astype(jnp.float32).astype(jnp.bfloat16)
        right = (lax.broadcasted_iota(jnp.int32, (wide, chunk), 0) == yk).astype(jnp.float32).astype(jnp.bfloat16)
        part = lax.dot_general(left, right, (((1,), (1,)), ((), ())), preferred_element_type=jnp.float32)
        if step == 0:
            acc_ref[...] = part
        else:
            acc_ref[...] += part
    rows = out_ref.shape[0]
    for block in range(tall // rows):
        out_ref[:, pl.ds(block * wide, wide)] = acc_ref[pl.ds(block * rows, rows), :].astype(jnp.bfloat16)


def build_slab(row, key, rows, keys):
    wide = 256
    edges = row.shape[0]
    chunk = 768 if edges % 768 == 0 else 128
    tall = rows * (keys // wide)
    xk = ((key // wide) * rows + row).reshape(1, edges)
    yk = (key % wide).reshape(1, edges)
    return pl.pallas_call(
        functools.partial(count_kernel, chunk),
        out_shape=jax.ShapeDtypeStruct((rows, keys), jnp.bfloat16),
        in_specs=[vmem(), vmem()],
        out_specs=vmem(),
        scratch_shapes=[pltpu.VMEM((tall, wide), jnp.float32)],
        compiler_params=pltpu.CompilerParams(vmem_limit_bytes=24 * MIB),
        name="count",
    )(xk, yk)


def select_own_kernel(per_part, idx_ref, own_ref, out_ref, made_ref, sem):
    members = own_ref.shape[0]
    for d in range(SEGMENT):
        for t in range(per_part):
            at = jnp.bitwise_and(idx_ref[d * 3 * per_part + per_part + t], members - 1)
            made_ref[d, t] = own_ref[at]
    copy = pltpu.make_async_copy(made_ref, out_ref, sem)
    copy.start()
    copy.wait()


def select_own(idx, own, per_part):
    shape = (SEGMENT, per_part) + own.shape[1:]
    return call(
        functools.partial(select_own_kernel, per_part),
        6,
        jax.ShapeDtypeStruct(shape, own.dtype),
        [smem(), vmem()],
        hbm(),
        [pltpu.VMEM(shape, own.dtype), pltpu.SemaphoreType.DMA],
    )(idx, own)


def select_far_kernel(per_part, idx_ref, first_ref, second_ref, out_ref, near_ref):
    members = first_ref.shape[0]
    near_ref[pl.ds(0, members)] = first_ref[...]
    near_ref[pl.ds(members, members)] = second_ref[...]
    for d in range(SEGMENT):
        for t in range(2 * per_part):
            place = t if t < per_part else t + per_part
            at = jnp.bitwise_and(idx_ref[d * 3 * per_part + place], 2 * members - 1)
            out_ref[d, t] = near_ref[at]


def select_far(idx, first, second, per_part):
    members = first.shape[0]
    return call(
        functools.partial(select_far_kernel, per_part),
        6,
        jax.ShapeDtypeStruct((SEGMENT, 2 * per_part) + first.shape[1:], first.dtype),
        [smem(), vmem(), vmem()],
        vmem(),
        [pltpu.VMEM((2 * members,) + first.shape[1:], first.dtype)],
    )(idx, first, second)


def layer_kernel(listed, slab_ref, xown_ref, xfar_ref, weight_ref, dinv_ref, bias_ref, cot_ref, hid_ref, part_ref):
    dinv = dinv_ref[...]
    per_part = listed // 3
    tall = 2 * SUB
    edge = xown_ref.shape[0] * tall
    rows = []
    for half in range(2):
        near = xown_ref[:, half].reshape(edge, LANE)
        far = xfar_ref[:, half].reshape(2 * edge, LANE)
        total = jnp.dot(slab_ref[:, :edge], near, preferred_element_type=jnp.float32)
        rows.append(total + jnp.dot(slab_ref[:, edge:], far, preferred_element_type=jnp.float32))
    gathered = jnp.concatenate(rows, axis=1)
    high = gathered.astype(jnp.bfloat16)
    low = (gathered - high.astype(jnp.float32)).astype(jnp.bfloat16)
    weight = weight_ref[...]
    total = jnp.dot(high, weight, preferred_element_type=jnp.float32)
    total = total + jnp.dot(low, weight, preferred_element_type=jnp.float32)
    pre = total * dinv + bias_ref[...]
    sig = jax.nn.sigmoid(pre)
    hid_ref[...] = (pre * sig).astype(hid_ref.dtype)
    grad_pre = cot_ref[...].astype(jnp.float32) * sig * (1.0 + pre * (1.0 - sig))
    back = (grad_pre * dinv).astype(jnp.bfloat16)
    contract = (((0,), (0,)), ((), ()))
    grad = lax.dot_general(high, back, contract, preferred_element_type=jnp.float32)
    grad = grad + lax.dot_general(low, back, contract, preferred_element_type=jnp.float32)
    sums = jnp.sum(grad_pre, axis=0, keepdims=True)
    sums_high = sums.astype(jnp.bfloat16).astype(jnp.float32)
    sums_low = sums - sums_high
    at = lax.broadcasted_iota(jnp.int32, (SUB, LANE), 0)
    extra = jnp.zeros((SUB, LANE), jnp.float32)
    for index, value in enumerate((sums_high, sums_low)):
        for half in range(2):
            lanes = slice(half * LANE, (half + 1) * LANE)
            extra = jnp.where(at == 2 * index + half, value[:, lanes], extra)
    extra = extra.astype(jnp.bfloat16)
    segments = grad.shape[0] // (SUB * SEGMENT)
    for half in range(2):
        lanes = slice(half * LANE, (half + 1) * LANE)
        partial = lax.dot_general(slab_ref[...], back[:, lanes], contract, preferred_element_type=jnp.float32)
        for holder in range(SEGMENT):
            at = holder * per_part * tall
            near = partial[at : at + per_part * tall].reshape(per_part, 2, SUB, LANE).astype(jnp.bfloat16)
            at = edge + 2 * at
            far = partial[at : at + 2 * per_part * tall].reshape(2 * per_part, 2, SUB, LANE).astype(jnp.bfloat16)
            for t in range(per_part):
                part_ref[holder, pl.ds(4 * t + 2 * half, 2)] = far[t]
                part_ref[holder, pl.ds(4 * (per_part + t) + 2 * half, 2)] = near[t]
                part_ref[holder, pl.ds(4 * (2 * per_part + t) + 2 * half, 2)] = far[per_part + t]
            part_ref[holder, 4 * listed] = extra
            for segment in range(segments):
                top = (segment * SEGMENT + holder) * SUB
                block = grad[top : top + SUB, lanes]
                part_ref[holder, 4 * listed + 1 + 2 * segment + half] = block.astype(jnp.bfloat16)


def layer(slab, xown, xfar, weight, dinv, bias, cotangent, listed):
    rows, width = cotangent.shape
    pieces = 4 * listed + 1 + 2 * (width // (SUB * SEGMENT))
    return call(
        functools.partial(layer_kernel, listed),
        16,
        (
            jax.ShapeDtypeStruct((rows, width), jnp.bfloat16),
            jax.ShapeDtypeStruct((SEGMENT, pieces, SUB, LANE), jnp.bfloat16),
        ),
        [vmem()] * 7,
        (vmem(), vmem()),
    )(slab, xown, xfar, weight, dinv, bias, cotangent)


def spread_kernel(got_ref, out_ref, made_ref, sem):
    total = got_ref[0]
    for segment in range(1, got_ref.shape[0]):
        total = total + got_ref[segment]
    top = total[0, 0:2] + total[0, 2:4]
    high = top.astype(jnp.bfloat16).astype(jnp.float32)
    low = top - high
    at = lax.broadcasted_iota(jnp.int32, (SUB, LANE), 0)
    piece = jnp.zeros((SUB, LANE), jnp.float32)
    for index in range(2):
        piece = jnp.where(at == index, high[index : index + 1], piece)
        piece = jnp.where(at == 2 + index, low[index : index + 1], piece)
    pieces = [piece.astype(jnp.bfloat16), total[1].astype(jnp.bfloat16), total[2].astype(jnp.bfloat16)]
    for ring in range(made_ref.shape[0]):
        for number, value in enumerate(pieces):
            made_ref[ring, number] = value
    copy = pltpu.make_async_copy(made_ref, out_ref, sem)
    copy.start()
    copy.wait()


def spread(got, rings):
    shape = (rings, 3, SUB, LANE)
    return call(
        spread_kernel,
        4,
        jax.ShapeDtypeStruct(shape, jnp.bfloat16),
        [vmem()],
        hbm(),
        [pltpu.VMEM(shape, jnp.bfloat16), pltpu.SemaphoreType.DMA],
    )(got)


def add_parts(per_part, parts, idx_ref, got_ref, acc_ref):
    acc_ref[...] = jnp.zeros_like(acc_ref)
    chains, tiles = acc_ref.shape[:2]
    for step in range(SEGMENT // chains):
        for part in parts:
            for t in range(part * per_part, (part + 1) * per_part):
                for j in range(chains):
                    d = step * chains + j
                    at = jnp.bitwise_and(idx_ref[d * 3 * per_part + t], tiles - 1)
                    acc_ref[j, at] += got_ref[d, pl.ds(4 * t, 4)].astype(jnp.float32)


def added(acc_ref, ref, number):
    part = pl.ds(number * ref.shape[0], ref.shape[0])
    value = acc_ref[0, part]
    for j in range(1, acc_ref.shape[0]):
        value = value + acc_ref[j, part]
    ref[...] = value.astype(ref.dtype)


def near_kernel(per_part, idx_ref, got_ref, first_ref, second_ref, out_ref, acc_ref, made_ref, sem):
    segments = made_ref.shape[0]
    extra = pl.ds(got_ref.shape[1] - 1 - 2 * segments, 1 + 2 * segments)
    total = got_ref[0, extra].astype(jnp.float32)
    for d in range(1, got_ref.shape[0]):
        total = total + got_ref[d, extra].astype(jnp.float32)
    for segment in range(segments):
        made_ref[segment, 0] = total[0]
        made_ref[segment, 1] = total[1 + 2 * segment]
        made_ref[segment, 2] = total[2 + 2 * segment]
    copy = pltpu.make_async_copy(made_ref, out_ref, sem)
    copy.start()
    add_parts(per_part, (0, 2), idx_ref, got_ref, acc_ref)
    added(acc_ref, first_ref, 0)
    added(acc_ref, second_ref, 1)
    copy.wait()


def collect_near(idx, got, members, per_part):
    piece = jax.ShapeDtypeStruct((members, 4, SUB, LANE), jnp.bfloat16)
    shape = (members // SEGMENT, 3, SUB, LANE)
    return call(
        functools.partial(near_kernel, per_part),
        8,
        (piece, piece, jax.ShapeDtypeStruct(shape, jnp.float32)),
        [smem(), vmem()],
        (vmem(), vmem(), hbm()),
        [
            pltpu.VMEM((2, 2 * members, 4, SUB, LANE), jnp.float32),
            pltpu.VMEM(shape, jnp.float32),
            pltpu.SemaphoreType.DMA,
        ],
    )(idx, got)


def own_kernel(per_part, idx_ref, got_ref, own_ref, acc_ref):
    add_parts(per_part, (1,), idx_ref, got_ref, acc_ref)
    added(acc_ref, own_ref, 0)


def collect_own(idx, got, members, per_part):
    return call(
        functools.partial(own_kernel, per_part),
        8,
        jax.ShapeDtypeStruct((members, 4, SUB, LANE), jnp.float32),
        [smem(), vmem()],
        vmem(),
        [pltpu.VMEM((2, members, 4, SUB, LANE), jnp.float32)],
    )(idx, got)


def join_kernel(own_ref, first_ref, second_ref, share_ref, out_ref, bias_ref):
    members = own_ref.shape[0]
    total = share_ref[0].astype(jnp.float32)
    for ring in range(1, share_ref.shape[0]):
        total = total + share_ref[ring].astype(jnp.float32)
    for half in range(2):
        bias_ref[:, half * LANE : (half + 1) * LANE] = total[0, half : half + 1] + total[0, half + 2 : half + 3]
    rows = [total[1].astype(jnp.bfloat16), total[2].astype(jnp.bfloat16)]
    for m in range(members):
        grad = own_ref[m] + first_ref[m].astype(jnp.float32) + second_ref[m].astype(jnp.float32)
        out_ref[m, pl.ds(0, 4)] = grad.astype(jnp.bfloat16)
        out_ref[m, 4] = rows[0]
        out_ref[m, 5] = rows[1]


def join(own, first, second, share):
    members = own.shape[0]
    return call(
        join_kernel,
        6,
        (
            jax.ShapeDtypeStruct((members, 6, SUB, LANE), jnp.bfloat16),
            jax.ShapeDtypeStruct((1, 2 * LANE), jnp.float32),
        ),
        [vmem()] * 4,
        (vmem(), vmem()),
    )(own, first, second, share)


def finish_kernel(final_ref, dinv_ref, weight_ref, features_ref, weight_grad_ref):
    members = final_ref.shape[0]
    dinv = dinv_ref[...]
    sides = []
    for half in range(2):
        pair = pl.ds(2 * half, 2)
        total = final_ref[pl.ds(0, SEGMENT), pair].astype(jnp.float32)
        for first in range(SEGMENT, members, SEGMENT):
            total = total + final_ref[pl.ds(first, SEGMENT), pair].astype(jnp.float32)
        sides.append(total.reshape(-1, LANE) * dinv)
    grad = jnp.concatenate(sides, axis=1).astype(jnp.bfloat16)
    features_ref[...] = lax.dot_general(
        grad, weight_ref[...], (((1,), (1,)), ((), ())), preferred_element_type=jnp.float32
    ).astype(features_ref.dtype)
    for half in range(2):
        rows = final_ref[:, 4 + half].astype(jnp.float32).reshape(-1, LANE)
        weight_grad_ref[:, half * LANE : (half + 1) * LANE] = rows


def finish(final, dinv, weight):
    width = weight.shape[0]
    rows = dinv.shape[0]
    return call(
        finish_kernel,
        6,
        (
            jax.ShapeDtypeStruct((rows, width), jnp.bfloat16),
            jax.ShapeDtypeStruct((width, width), jnp.float32),
        ),
        [vmem()] * 3,
        (vmem(), vmem()),
    )(final, dinv, weight)


def swap(x, axis):
    return lax.all_to_all(x, axis, 0, 0, tiled=True)


def segment_swap(x, members):
    groups = [list(range(first, first + SEGMENT)) for first in range(0, members, SEGMENT)]
    return lax.all_to_all(x, "grp", 0, 0, axis_index_groups=groups, tiled=True)


def across_swap(x, members):
    groups = [list(range(first, members, SEGMENT)) for first in range(SEGMENT)]
    return lax.all_to_all(x, "grp", 0, 0, axis_index_groups=groups, tiled=True)


def per_device(features, weight, bias, cotangent, degree, tile_cols, edge_tile, edge_row, edge_col):
    rows, _ = features.shape
    members = lax.axis_size("grp")
    rings = lax.axis_size("rep")
    listed = tile_cols.shape[1]
    per_part = listed // 3

    payload, dinv = cut(features, degree[None, :], tile_cols)
    got = swap(payload, "grp")
    own = got[:, :4]
    first = with_partner(own, "rep")
    second = with_other(own, "rep")

    names = got[:, 4, 0, :listed].astype(jnp.int32)
    part = lax.broadcasted_iota(jnp.int32, names.shape, 1) // per_part
    even = lax.axis_index("rep") % 2 == 0
    late = jnp.where(even, part == 0, part == 2)
    idx = names % members + jnp.where(late, members, 0)
    segment = lax.axis_index("grp") // SEGMENT
    idx = idx.reshape(-1)
    near_idx = lax.dynamic_slice_in_dim(idx, segment * SEGMENT * listed, SEGMENT * listed, 0)

    tile = edge_tile[0]
    col = edge_col[0]
    tall = 2 * SUB
    far_tile = jnp.where(tile < per_part, tile, tile - per_part)
    is_own = (tile >= per_part) & (tile < 2 * per_part)
    own_key = (col // tall * per_part + tile - per_part) * tall
    far_key = per_part * rows + (col // tall * 2 * per_part + far_tile) * tall
    key = jnp.where(is_own, own_key, far_key) + col % tall
    slab = build_slab(edge_row[0], key, rows, listed * rows)

    chosen_own = select_own(near_idx, own, per_part)
    window_own = segment_swap(chosen_own, members)
    window_far = segment_swap(select_far(near_idx, first, second, per_part), members)
    hidden, partial = layer(
        slab,
        window_own.reshape(rows // tall * per_part, 2, tall, LANE),
        window_far.reshape(rows // tall * 2 * per_part, 2, tall, LANE),
        weight,
        dinv,
        bias[None, :],
        cotangent,
        listed,
    )
    mine = segment_swap(partial, members)
    to_first, to_second, grad = collect_near(near_idx, mine, members, per_part)
    grad = across_swap(grad, members)
    share = spread(grad, rings)
    share = swap(share, "rep")
    from_first = with_partner(to_first, "rep")
    from_second = with_other(to_second, "rep")
    own_sum = collect_own(near_idx, mine, members, per_part)

    final, grad_bias = join(own_sum, from_first, from_second, share)
    final = swap(final, "grp")
    grad_features, grad_weight = finish(final, dinv, weight)
    return (hidden, grad_features, grad_weight, grad_bias[0])


def solution(mesh):
    return jax.shard_map(
        per_device,
        mesh=mesh,
        in_specs=(
            P(("rep", "grp"), None),
            P(),
            P(),
            P(("rep", "grp"), None),
            P(("rep", "grp")),
            P(("rep", "grp"), None),
            P(("rep", "grp"), None),
            P(("rep", "grp"), None),
            P(("rep", "grp"), None),
        ),
        out_specs=(P(("rep", "grp"), None), P(("rep", "grp"), None), P(), P()),
        check_vma=False,
    )
```
